128 devices in a mesh: slab: 4 (over x), member: 32 (over y, z, core).
Axes of the slice: x: 4, y: 4, z: 4, core: 2. Of those that a mesh axis runs over, the one named last changes fastest.
Arguments:
- initial: float32 [256, 512, 1024], P('member', 'slab'), may hold values from -6 to 6
- stencil_numbers: float32 [3, 512, 1024], P(None, 'slab'), may hold values from -0.25 to 0.25, as said below
- innovations: float32 [256, 131072], P(None, ('slab', 'member')), may hold values from -6 to 6
- obs_prec: float32 [131072], P(('slab', 'member')), may hold values from 0.05 to 0.5
- obs_cell: int32 [4096, 32], P(('slab', 'member')), may hold values from 0 to 127
- band_idx: int32 [4096, 9], P(('slab', 'member')), may hold values from 0 to 4095, as said below
Outputs:
- analysis: float32 [256, 512, 1024], P('member', 'slab')
The draws below stay inside these ranges and needn't reach their ends.
Inputs may be any that keep to these rules, and one draw needn't show every extreme that they name: stencil_numbers[0] lies in 0.08 to 0.2; stencil_numbers[1] and stencil_numbers[2] lie in -0.25 to 0.25. `band_idx`: row b holds 9 distinct block indices j with |j - b| <= 8.
All inputs are finite; a program needn't handle non-finite values.
Results may differ from the reference program's by a relative error of at most 0.00011.
Values sent between devices are 32-bit elements; how exact they have to be, the bound alone decides.
A program may use at most 128 MiB of HBM per device.

```python
import math
import jax
import jax.numpy as jnp
from jax import lax

LON = 1024
MEM_DEV = 8
STEPS = 4
OB = 32
R = 8
BAND = 9
NLAT = 512
REALIZATIONS = 256
TILE_TOTAL = 4096
NOBS = 131072
N_MEMBER = 32


def draw_stencil_numbers(key, part):
    key_diff, key_flow = jax.random.split(key)
    diffusion = jax.random.uniform(key_diff, (1, NLAT, LON), jnp.float32, 0.08, 0.2)
    flows = jax.random.uniform(key_flow, (2, NLAT, LON), jnp.float32, -0.25, 0.25)
    return jnp.concatenate([diffusion, flows], axis=0)


def draw_band_idx(key, part):
    width = 2 * R + 1
    offsets = jnp.arange(width, dtype=jnp.int32) - R
    blocks = jnp.arange(TILE_TOTAL, dtype=jnp.int32)[:, None] + offsets[None, :]
    is_valid = (blocks >= 0) & (blocks < TILE_TOTAL)
    scores = jax.random.randint(key, (TILE_TOTAL, width), 0, 1000, dtype=jnp.int32) * width + jnp.arange(width, dtype=jnp.int32)[None, :]
    scores = jnp.where(is_valid, scores + 1, -1)
    best_scores, positions = lax.top_k(scores, BAND)
    return jnp.take_along_axis(blocks, positions, axis=1).astype(jnp.int32)


def touch_ends(array, own_key, least, high):
    spot = [jax.random.randint(jax.random.fold_in(own_key, axis), (), 0, length) for axis, length in enumerate(array.shape)]
    main_axis = array.shape.index(max(array.shape))
    next_to = spot[:main_axis] + [(spot[main_axis] + 1) % array.shape[main_axis]] + spot[main_axis + 1:]
    return array.at[tuple(spot)].set(least).at[tuple(next_to)].set(high)


def steps_of(key, extent, cuts, low, high):
    loudness, own = 1.0, jax.random.fold_in(key, 6)
    for dim, parts in cuts:
        heights = jnp.exp(jax.random.uniform(jax.random.fold_in(own, dim), (parts,), jnp.float32, low / len(cuts), high / len(cuts)))
        loudness = loudness * jnp.repeat(heights, extent[dim] // parts).reshape([-1 if axis == dim else 1 for axis in range(len(extent))])
    return loudness


def noise(stream_key, dims, scale, limit, cuts=(), held_as=jnp.bfloat16):
    drawn = scale * jax.random.normal(stream_key, dims, jnp.float32)
    if cuts:
        drawn = drawn * steps_of(stream_key, dims, cuts, -0.22, 0.18)
    return jnp.clip(drawn, -limit, limit).astype(held_as)


def setup_inputs(seed: int = 0) -> dict:
    seeds = jax.random.split(jax.random.key(seed), 7)
    initial = noise(seeds[0], (REALIZATIONS, NLAT, LON), 1.0, 6.0, ((0, 32), (1, 4)), jnp.float32)
    stencil_numbers = draw_stencil_numbers(jax.random.fold_in(seeds[6], 71), 0)
    innovations = noise(seeds[2], (REALIZATIONS, NOBS), 1.0, 6.0, ((1, 128),), jnp.float32)
    obs_prec = jnp.clip(jnp.exp(math.log(0.5) - 2.3025851 * jax.random.uniform(seeds[3], (NOBS,), jnp.float32) ** steps_of(seeds[3], (NOBS,), ((0, 128),), -0.2, 0.2)), 0.05, 0.5)
    obs_cell = touch_ends(jax.random.randint(seeds[4], (TILE_TOTAL, OB), 0, 128), jax.random.fold_in(seeds[4], 1), 0, 127).astype(jnp.int32)
    band_idx = draw_band_idx(jax.random.fold_in(seeds[6], 71), 0)
    return {"initial": initial, "stencil_numbers": stencil_numbers, "innovations": innovations, "obs_prec": obs_prec, "obs_cell": obs_cell, "band_idx": band_idx}


exact = lax.Precision.HIGHEST


def advance(padded, stencil_numbers):
    centre = padded[:, 1:-1, :]
    north_cell = padded[:, 2:, :]
    south_cell = padded[:, :-2, :]
    east_cell = jnp.roll(centre, -1, axis=2)
    west_cell = jnp.roll(centre, 1, axis=2)
    spread = east_cell + west_cell + north_cell + south_cell - 4.0 * centre
    return centre + stencil_numbers[0] * spread - 0.5 * stencil_numbers[1] * (east_cell - west_cell) - 0.5 * stencil_numbers[2] * (north_cell - south_cell)


def batched_propagation(realization_batch, stencil_numbers):
    fields = realization_batch
    for step_no in range(STEPS):
        fields = advance(jnp.pad(fields, ((0, 0), (1, 1), (0, 0))), stencil_numbers)
    return fields


def reference(initial, stencil_numbers, innovations, obs_prec, obs_cell, band_idx):
    realization_pieces = initial.reshape(N_MEMBER, MEM_DEV, NLAT, LON)
    propagation_operator = lax.map(lambda realization_batch: batched_propagation(realization_batch, stencil_numbers), realization_pieces)
    partition_shape = propagation_operator.reshape(REALIZATIONS, TILE_TOTAL, 128)
    ensemble_mean = jnp.mean(partition_shape, axis=0)
    anomaly = partition_shape - ensemble_mean
    observed = jnp.take_along_axis(anomaly, obs_cell[None, :, :], axis=2)
    weighted = innovations.reshape(REALIZATIONS, TILE_TOTAL, OB) * obs_prec.reshape(TILE_TOTAL, OB)

    def one_block(block_no):
        band_rows = band_idx[block_no]
        distance = jnp.abs(band_rows - block_no).astype(jnp.float32)
        tapers = 1.0 - distance / (R + 1.0)
        obs_band = (observed[:, band_rows, :] * tapers[None, :, None]).reshape(REALIZATIONS, BAND * OB)
        inn_band = weighted[:, band_rows, :].reshape(REALIZATIONS, BAND * OB)
        cells = lax.dynamic_index_in_dim(anomaly, block_no, axis=1, keepdims=False)
        cross_cov = jnp.dot(obs_band.T, cells, precision=exact, preferred_element_type=jnp.float32)
        return jnp.dot(inn_band, cross_cov, precision=exact, preferred_element_type=jnp.float32) / (REALIZATIONS - 1)

    increment = lax.map(one_block, jnp.arange(TILE_TOTAL, dtype=jnp.int32))
    increment = jnp.transpose(increment, (1, 0, 2))
    return (partition_shape + increment).reshape(REALIZATIONS, NLAT, LON)
```

```python
import functools

import jax
import jax.numpy as jnp
from jax import lax
from jax.experimental import pallas as pl
from jax.experimental.pallas import tpu as pltpu
from jax.sharding import PartitionSpec as P

MESH = pl.DeviceIdType.MESH
F32 = jnp.float32
BF16 = jnp.bfloat16
OB = 32
R = 8
SLABS = 4
GROUPS = 32
CHIPS = 16
ROWS = 128
LON = 1024
MEM = 8
MEMBERS = 256
TILE_ROWS = 4
ROW_BLOCKS = 8
TILE_BLOCKS = 32
ROW_OBS = ROW_BLOCKS * OB


def split(value):
    high = value.astype(BF16)
    low = (value - high.astype(F32)).astype(BF16)
    return high, low


def dot3(a_high, a_low, b_high, b_low):
    dot = functools.partial(jnp.dot, preferred_element_type=F32)
    return dot(a_high, b_high) + dot(a_high, b_low) + dot(a_low, b_high)


def dot_t(a, b):
    return lax.dot_general(a, b, (((1,), (1,)), ((), ())), preferred_element_type=F32)


def cycle_kernel(
    init_ref, sten_ref, inn_ref, prec_ref, cell_ref, band_ref, ret_ref,
    xbuf, xt, sten, coef, step_a, step_b, fsend, fields, anom_high, anom_low,
    pick, obs, obs_high, obs_low, wgt, wgt_high, wgt_low, inn, taper, upd,
    load_sem, halo_send, halo_recv, fwd_send, fwd_recv, own_sem, rim_send, rim_recv, ret_send, ret_recv,
):
    s = lax.axis_index("slab")
    g = lax.axis_index("member")
    chip = g // 2
    core = g % 2
    flat = s * GROUPS + g
    up = lax.rem(s + 1, SLABS)
    down = lax.rem(s + SLABS - 1, SLABS)
    nxt = lax.rem(flat + 1, SLABS * GROUPS)
    prv = lax.rem(flat + SLABS * GROUPS - 1, SLABS * GROUPS)
    nxt_id = (nxt // GROUPS, lax.rem(nxt, GROUPS))
    prv_id = (prv // GROUPS, lax.rem(prv, GROUPS))

    barrier = pltpu.get_barrier_semaphore()

    def greet(i, carry):
        peer = lax.rem(g + i, GROUPS)
        pl.semaphore_signal(barrier, inc=1, device_id=(s, peer), device_id_type=MESH)
        return carry

    for device in ((up, g), (down, g), nxt_id, prv_id):
        pl.semaphore_signal(barrier, inc=1, device_id=device, device_id_type=MESH)
    lax.fori_loop(1, GROUPS, greet, 0)

    load_x = pltpu.make_async_copy(init_ref, xbuf, load_sem.at[0])
    load_s = pltpu.make_async_copy(sten_ref, sten.at[:, pl.ds(8, ROWS), :], load_sem.at[1])
    load_i = pltpu.make_async_copy(inn_ref, inn, load_sem.at[2])
    load_x.start()
    load_s.start()
    load_i.start()

    load_x.wait()

    def turn(k, carry):
        start = pl.multiple_of(k * 8, 8)
        rows = xbuf[:, pl.ds(start, 8), :]
        xt[pl.ds(k * 8 + 4, 8)] = jnp.swapaxes(rows, 0, 1)
        return carry

    turn(0, 0)
    turn(CHIPS - 1, 0)

    pl.semaphore_wait(barrier, GROUPS - 1 + 4)

    def remote(src, dst, send_sem, recv_sem, device):
        return pltpu.make_async_remote_copy(
            src_ref=src, dst_ref=dst, send_sem=send_sem, recv_sem=recv_sem,
            device_id=device, device_id_type=MESH,
        )

    halos = [
        remote(sten_ref.at[:, pl.ds(ROWS - 8, 8), :], sten.at[:, pl.ds(0, 8), :], halo_send.at[0], halo_recv.at[0], (up, g)),
        remote(sten_ref.at[:, pl.ds(0, 8), :], sten.at[:, pl.ds(ROWS + 8, 8), :], halo_send.at[1], halo_recv.at[1], (down, g)),
        remote(xt.at[pl.ds(ROWS, 4)], xt.at[pl.ds(0, 4)], halo_send.at[2], halo_recv.at[2], (up, g)),
        remote(xt.at[pl.ds(4, 4)], xt.at[pl.ds(ROWS + 4, 4)], halo_send.at[3], halo_recv.at[3], (down, g)),
    ]
    for copy in halos:
        copy.start()

    lax.fori_loop(1, CHIPS - 1, turn, 0)

    def coefficients(start, live):
        rows = pl.ds(start, 8)
        k = sten[0, rows, :] * live
        u = sten[1, rows, :] * (0.5 * live)
        v = sten[2, rows, :] * (0.5 * live)
        coef[0, rows, :] = 1.0 - 4.0 * k
        coef[1, rows, :] = k - u
        coef[2, rows, :] = k + u
        coef[3, rows, :] = k - v
        coef[4, rows, :] = k + v

    load_s.wait()

    def own_coefficients(t, carry):
        coefficients(pl.multiple_of(t * 8 + 8, 8), 1.0)
        return carry

    lax.fori_loop(0, CHIPS, own_coefficients, 0)

    def target(i):
        return lax.rem(chip + 7 * i, CHIPS)

    def early_target(i):
        k = target(i)
        edge = 1 - (lax.rem(k + 1, CHIPS) + 14) // 16
        middle = 1 - (lax.rem(k + 9, CHIPS) + 14) // 16
        first = 1 - (i + 11) // 16
        later = ((i + 7) // 16) * (1 - (i + 3) // 16)
        return lax.rem(k + 8 * (first * edge + later * middle), CHIPS)

    def advance(src, src_start, dst, dst_start, count, coef_base, coef_offset):
        for row in range(count):
            centre = src[src_start + row + 1]
            north = src[src_start + row + 2]
            south = src[src_start + row]
            east = pltpu.roll(centre, LON - 1, 1)
            west = pltpu.roll(centre, 1, 1)
            at = pl.ds(coef_base + coef_offset + row, 1)
            dst[dst_start + row] = (
                coef[0, at, :] * centre
                + coef[1, at, :] * east
                + coef[2, at, :] * west
                + coef[3, at, :] * north
                + coef[4, at, :] * south
            )

    def forecast(k):
        base = pl.multiple_of(k * 8, 8)
        advance(xt, k * 8, step_a, 0, 14, base, 5)
        advance(step_a, 0, step_b, 0, 12, base, 6)
        advance(step_b, 0, step_a, 0, 10, base, 7)
        advance(step_a, 0, fsend, k * 8, 8, base, 8)

    def send_rows(k, c, row, count, sem):
        remote(
            fsend.at[pl.ds(k * 8 + 4 * c + row, count)],
            fields.at[pl.ds(row, count), pl.ds(pl.multiple_of(g * MEM, MEM), MEM), :],
            fwd_send, sem, (s, 2 * k + c),
        ).start()

    def first_rows(i, carry):
        @pl.when(i == 5)
        def _():
            for copy in halos:
                copy.wait()
            coefficients(0, jnp.where(s == 0, 0.0, 1.0).astype(F32))
            coefficients(ROWS + 8, jnp.where(s == SLABS - 1, 0.0, 1.0).astype(F32))

            @pl.when(s == 0)
            def _():
                xt[pl.ds(0, 4)] = jnp.zeros((4, MEM, LON), F32)

            @pl.when(s == SLABS - 1)
            def _():
                xt[pl.ds(ROWS + 4, 4)] = jnp.zeros((4, MEM, LON), F32)

        k = early_target(i)
        forecast(k)
        for c in range(2):
            send_rows(k, c, 0, 2, fwd_recv.at[0])
        return carry

    lax.fori_loop(1, CHIPS, first_rows, 0)
    forecast(chip)
    send_rows(chip, 1 - core, 0, 2, fwd_recv.at[0])
    own = pltpu.make_async_copy(
        fsend.at[pl.ds(g * 4, 4)], fields.at[:, pl.ds(pl.multiple_of(g * MEM, MEM), MEM), :], own_sem.at[0]
    )
    own.start()

    for row in (2, 3):
        def later_rows(i, carry, row=row):
            k = target(i)
            for c in range(2):
                send_rows(k, c, row, 1, fwd_recv.at[row - 1])
            return carry

        lax.fori_loop(1, CHIPS, later_rows, 0)
        send_rows(chip, 1 - core, row, 1, fwd_recv.at[row - 1])

    load_i.wait()
    scale = 1.0 / ((R + 1.0) * (MEMBERS - 1.0))
    for row in range(TILE_ROWS):
        cols = pl.ds(row * ROW_OBS, ROW_OBS)
        wgt[row + 1] = inn[:, cols] * (prec_ref[:, cols] * scale)

    def split_weights(slot):
        wgt_high[slot], wgt_low[slot] = split(wgt[slot])

    def split_observed(slot):
        obs_high[slot], obs_low[slot] = split(obs[slot])

    rim_w = [
        remote(wgt.at[TILE_ROWS], wgt.at[0], rim_send.at[0], rim_recv.at[0], nxt_id),
        remote(wgt.at[1], wgt.at[TILE_ROWS + 1], rim_send.at[1], rim_recv.at[1], prv_id),
    ]
    for copy in rim_w:
        copy.start()
    rim_o = [
        remote(obs.at[TILE_ROWS], obs.at[0], rim_send.at[2], rim_recv.at[2], nxt_id),
        remote(obs.at[1], obs.at[TILE_ROWS + 1], rim_send.at[3], rim_recv.at[3], prv_id),
    ]

    for row in range(TILE_ROWS):
        split_weights(row + 1)

    lane = lax.broadcasted_iota(jnp.int32, (OB, 128), 1)
    for b in range(TILE_BLOCKS):
        pick[b] = jnp.where(lane == cell_ref[:, b : b + 1], 1.0, 0.0).astype(BF16)

    block = lax.broadcasted_iota(jnp.int32, (TILE_BLOCKS, 128), 0)
    slot_lane = lax.broadcasted_iota(jnp.int32, (TILE_BLOCKS, 128), 1)
    here = flat * TILE_BLOCKS + block
    row_start = flat * TILE_BLOCKS + jnp.bitwise_and(block, -8) - R
    total = jnp.zeros((TILE_BLOCKS, 128), F32)
    for n in range(R + 1):
        member_of = band_ref[:, n : n + 1]
        height = (R + 1.0) - jnp.abs(member_of - here).astype(F32)
        total = total + jnp.where(slot_lane == member_of - row_start, height, 0.0)
    taper[...] = total

    own.wait()

    def prepare(row):
        def columns(c, carry):
            cols = pl.ds(pl.multiple_of(c * 256, 256), 256)
            field = fields[row, :, cols]
            mean = jnp.sum(field, axis=0, keepdims=True) * (1.0 / MEMBERS)
            high, low = split(field - mean)
            anom_high[row, :, cols] = high
            anom_low[row, :, cols] = low
            for b in range(2):
                pair = pl.ds(pl.multiple_of(c * 64 + b * OB, OB), OB)
                chosen = pick[row * ROW_BLOCKS + c * 2 + b]
                part = slice(b * 128, b * 128 + 128)
                obs[row + 1, pair, :] = dot_t(chosen, high[:, part]) + dot_t(chosen, low[:, part])
            return carry

        lax.fori_loop(0, 4, columns, 0)
        split_observed(row + 1)

    def arrived(row, count, sem):
        view = fields.at[pl.ds(row, count), pl.ds(0, MEMBERS - MEM), :]
        pltpu.make_async_copy(view, view, sem).wait()

    def analyse(row):
        def columns(c, carry):
            cols = pl.ds(pl.multiple_of(c * 256, 256), 256)
            high = anom_high[row, :, cols]
            low = anom_low[row, :, cols]
            weights = [taper[pl.ds(row * ROW_BLOCKS + c * 2 + b, 1), :] for b in range(2)]
            total = fields[row, :, cols]
            for part in range(3):
                slot = row + part
                cross = dot3(obs_high[slot], obs_low[slot], high, low)
                spread = jnp.concatenate(
                    [
                        jnp.concatenate(
                            [
                                jnp.broadcast_to(weights[b][:, part * 8 + j : part * 8 + j + 1], (OB, 128))
                                for b in range(2)
                            ],
                            axis=1,
                        )
                        for j in range(8)
                    ],
                    axis=0,
                )
                cross_high, cross_low = split(cross * spread)
                total = total + dot3(wgt_high[slot], wgt_low[slot], cross_high, cross_low)
            upd[row, :, cols] = total
            return carry

        lax.fori_loop(0, 4, columns, 0)

    def give_back(row):
        def one(k, c):
            d = 2 * k + c
            remote(
                upd.at[row, pl.ds(pl.multiple_of(d * MEM, MEM), MEM), :], ret_ref.at[TILE_ROWS * g + row],
                ret_send, ret_recv, (s, d),
            ).start()

        def others(i, carry):
            k = target(i)
            for c in range(2):
                one(k, c)
            return carry

        lax.fori_loop(1, CHIPS, others, 0)
        one(chip, 1 - core)

    arrived(0, 2, fwd_recv.at[0])
    prepare(0)
    rim_o[1].start()
    prepare(1)
    arrived(2, 1, fwd_recv.at[1])
    prepare(2)

    def finish(t, carry):
        row = lax.rem(t + 1, TILE_ROWS)

        @pl.when(t == 1)
        def _():
            arrived(3, 1, fwd_recv.at[2])
            prepare(3)
            rim_o[0].start()

        @pl.when(t == 2)
        def _():
            rim_w[1].wait_recv()
            rim_o[1].wait_recv()
            split_weights(TILE_ROWS + 1)
            split_observed(TILE_ROWS + 1)

        @pl.when(t == 3)
        def _():
            rim_w[0].wait_recv()
            rim_o[0].wait_recv()
            split_weights(0)
            split_observed(0)

        analyse(row)
        give_back(row)
        return carry

    lax.fori_loop(0, TILE_ROWS, finish, 0)

    keep = pltpu.make_async_copy(
        upd.at[:, pl.ds(pl.multiple_of(g * MEM, MEM), MEM), :], ret_ref.at[pl.ds(TILE_ROWS * g, TILE_ROWS)], own_sem.at[1]
    )
    keep.start()
    for copy in rim_w + rim_o:
        copy.wait_send()
    sent = fsend.at[pl.ds(0, ROWS - 4)]
    pltpu.make_async_copy(sent, sent, fwd_send).wait()
    keep.wait()
    back = ret_ref.at[pl.ds(0, ROWS - 4)]
    pltpu.make_async_copy(back, back, ret_send).wait()
    pltpu.make_async_copy(back, back, ret_recv).wait()


def turn_kernel(rows_ref, out_ref):
    out_ref[...] = jnp.swapaxes(rows_ref[...], 0, 1)


def shards(initial, stencil_numbers, innovations, obs_prec, obs_cell, band_idx):
    vmem = pl.BlockSpec(memory_space=pltpu.VMEM)
    hbm = pl.BlockSpec(memory_space=pl.ANY)
    dma = pltpu.SemaphoreType.DMA
    rows = pl.pallas_call(
        cycle_kernel,
        out_shape=jax.ShapeDtypeStruct((ROWS, MEM, LON), F32),
        in_specs=[hbm, hbm, hbm, vmem, vmem, vmem],
        out_specs=hbm,
        scratch_shapes=[
            pltpu.VMEM((MEM, ROWS, LON), F32),
            pltpu.VMEM((ROWS + 8, MEM, LON), F32),
            pltpu.VMEM((3, ROWS + 16, LON), F32),
            pltpu.VMEM((5, ROWS + 16, LON), F32),
            pltpu.VMEM((14, MEM, LON), F32),
            pltpu.VMEM((14, MEM, LON), F32),
            pltpu.VMEM((ROWS, MEM, LON), F32),
            pltpu.VMEM((TILE_ROWS, MEMBERS, LON), F32),
            pltpu.VMEM((TILE_ROWS, MEMBERS, LON), BF16),
            pltpu.VMEM((TILE_ROWS, MEMBERS, LON), BF16),
            pltpu.VMEM((TILE_BLOCKS, OB, 128), BF16),
            pltpu.VMEM((TILE_ROWS + 2, ROW_OBS, MEMBERS), F32),
            pltpu.VMEM((TILE_ROWS + 2, ROW_OBS, MEMBERS), BF16),
            pltpu.VMEM((TILE_ROWS + 2, ROW_OBS, MEMBERS), BF16),
            pltpu.VMEM((TILE_ROWS + 2, MEMBERS, ROW_OBS), F32),
            pltpu.VMEM((TILE_ROWS + 2, MEMBERS, ROW_OBS), BF16),
            pltpu.VMEM((TILE_ROWS + 2, MEMBERS, ROW_OBS), BF16),
            pltpu.VMEM((MEMBERS, TILE_ROWS * ROW_OBS), F32),
            pltpu.VMEM((TILE_BLOCKS, 128), F32),
            pltpu.VMEM((TILE_ROWS, MEMBERS, LON), F32),
            dma((3,)),
            dma((4,)),
            dma((4,)),
            dma(()),
            dma((3,)),
            dma((2,)),
            dma((4,)),
            dma((4,)),
            dma(()),
            dma(()),
        ],
        compiler_params=pltpu.CompilerParams(
            collective_id=0, has_side_effects=True, vmem_limit_bytes=60 * 2**20
        ),
        name="cycle",
    )(initial, stencil_numbers, innovations, obs_prec.reshape(1, -1), obs_cell.T, band_idx)
    group = 32
    return pl.pallas_call(
        turn_kernel,
        grid=(ROWS // group,),
        out_shape=jax.ShapeDtypeStruct((MEM, ROWS, LON), F32),
        in_specs=[pl.BlockSpec((group, MEM, LON), lambda i: (i, 0, 0))],
        out_specs=pl.BlockSpec((MEM, group, LON), lambda i: (0, i, 0)),
        compiler_params=pltpu.CompilerParams(vmem_limit_bytes=32 * 2**20),
        name="turn",
    )(rows)


def solution(mesh):
    in_specs = (
        P("member", "slab", None),
        P(None, "slab", None),
        P(None, ("slab", "member")),
        P(("slab", "member")),
        P(("slab", "member"), None),
        P(("slab", "member"), None),
    )
    out_specs = P("member", "slab", None)
    return jax.shard_map(shards, mesh=mesh, in_specs=in_specs, out_specs=out_specs, check_vma=False)
```

```python
import functools

import jax
import jax.numpy as jnp
from jax import lax
from jax.experimental import pallas as pl
from jax.experimental.pallas import tpu as pltpu
from jax.sharding import PartitionSpec as P

MESH = pl.DeviceIdType.MESH
F32 = jnp.float32
BF16 = jnp.bfloat16
OB = 32
R = 8
SLABS = 4
GROUPS = 32
CHIPS = 16
ROWS = 128
LON = 1024
MEM = 8
MEMBERS = 256
TILE_ROWS = 4
ROW_BLOCKS = 8
TILE_BLOCKS = 32
ROW_OBS = ROW_BLOCKS * OB


def split(value):
    high = value.astype(BF16)
    low = (value - high.astype(F32)).astype(BF16)
    return high, low


def dot3(a_high, a_low, b_high, b_low):
    dot = functools.partial(jnp.dot, preferred_element_type=F32)
    return dot(a_high, b_high) + dot(a_high, b_low) + dot(a_low, b_high)


def dot_t(a, b):
    return lax.dot_general(a, b, (((1,), (1,)), ((), ())), preferred_element_type=F32)


def cycle_kernel(
    init_ref, sten_ref, inn_ref, prec_ref, cell_ref, band_ref, ret_ref,
    xbuf, xt, sten, coef, step_a, step_b, fsend, fields, anom_high, anom_low,
    pick, obs, obs_high, obs_low, wgt, wgt_high, wgt_low, inn, square, taper, upd,
    load_sem, halo_send, halo_recv, fwd_send, fwd_recv, own_sem, rim_send, rim_recv, ret_send, ret_recv,
):
    s = lax.axis_index("slab")
    g = lax.axis_index("member")
    chip = g // 2
    core = g % 2
    flat = s * GROUPS + g
    up = lax.rem(s + 1, SLABS)
    down = lax.rem(s + SLABS - 1, SLABS)
    nxt = lax.rem(flat + 1, SLABS * GROUPS)
    prv = lax.rem(flat + SLABS * GROUPS - 1, SLABS * GROUPS)
    nxt_id = (nxt // GROUPS, lax.rem(nxt, GROUPS))
    prv_id = (prv // GROUPS, lax.rem(prv, GROUPS))

    barrier = pltpu.get_barrier_semaphore()

    def greet(i, carry):
        peer = lax.rem(g + i, GROUPS)
        pl.semaphore_signal(barrier, inc=1, device_id=(s, peer), device_id_type=MESH)
        return carry

    for device in ((up, g), (down, g), nxt_id, prv_id):
        pl.semaphore_signal(barrier, inc=1, device_id=device, device_id_type=MESH)
    lax.fori_loop(1, GROUPS, greet, 0)

    load_x = pltpu.make_async_copy(init_ref, xbuf, load_sem.at[0])
    load_s = pltpu.make_async_copy(sten_ref, sten.at[:, pl.ds(8, ROWS), :], load_sem.at[1])
    load_i = pltpu.make_async_copy(inn_ref, inn, load_sem.at[2])
    load_x.start()
    load_s.start()
    load_i.start()

    load_x.wait()

    def turn(k, carry):
        start = pl.multiple_of(k * 8, 8)
        rows = xbuf[:, pl.ds(start, 8), :]
        xt[pl.ds(k * 8 + 4, 8)] = jnp.swapaxes(rows, 0, 1)
        return carry

    lax.fori_loop(0, CHIPS, turn, 0)

    def coefficients(start, live):
        rows = pl.ds(start, 8)
        k = sten[0, rows, :] * live
        u = sten[1, rows, :] * (0.5 * live)
        v = sten[2, rows, :] * (0.5 * live)
        coef[0, rows, :] = 1.0 - 4.0 * k
        coef[1, rows, :] = k - u
        coef[2, rows, :] = k + u
        coef[3, rows, :] = k - v
        coef[4, rows, :] = k + v

    load_s.wait()

    def own_coefficients(t, carry):
        coefficients(pl.multiple_of(t * 8 + 8, 8), 1.0)
        return carry

    lax.fori_loop(0, CHIPS, own_coefficients, 0)

    def remote(src, dst, send_sem, recv_sem, device):
        return pltpu.make_async_remote_copy(
            src_ref=src, dst_ref=dst, send_sem=send_sem, recv_sem=recv_sem,
            device_id=device, device_id_type=MESH,
        )

    halos = [
        remote(sten_ref.at[:, pl.ds(ROWS - 8, 8), :], sten.at[:, pl.ds(0, 8), :], halo_send.at[0], halo_recv.at[0], (up, g)),
        remote(sten_ref.at[:, pl.ds(0, 8), :], sten.at[:, pl.ds(ROWS + 8, 8), :], halo_send.at[1], halo_recv.at[1], (down, g)),
        remote(xt.at[pl.ds(ROWS, 4)], xt.at[pl.ds(0, 4)], halo_send.at[2], halo_recv.at[2], (up, g)),
        remote(xt.at[pl.ds(4, 4)], xt.at[pl.ds(ROWS + 4, 4)], halo_send.at[3], halo_recv.at[3], (down, g)),
    ]

    def target(i):
        d = lax.rem(7 * i, CHIPS)
        return lax.rem(chip // 4 + d // 4, 4) * 4 + lax.rem(lax.rem(chip, 4) + lax.rem(d, 4), 4)

    def early_target(i):
        k = target(i)
        edge = 1 - (lax.rem(k + 1, CHIPS) + 14) // 16
        middle = 1 - (lax.rem(k + 9, CHIPS) + 14) // 16
        first = 1 - (i + 11) // 16
        later = ((i + 7) // 16) * (1 - (i + 3) // 16)
        return lax.rem(k + 8 * (first * edge + later * middle), CHIPS)

    def advance(src, src_start, dst, dst_start, count, coef_base, coef_offset):
        for row in range(count):
            centre = src[src_start + row + 1]
            north = src[src_start + row + 2]
            south = src[src_start + row]
            east = pltpu.roll(centre, LON - 1, 1)
            west = pltpu.roll(centre, 1, 1)
            at = pl.ds(coef_base + coef_offset + row, 1)
            dst[dst_start + row] = (
                coef[0, at, :] * centre
                + coef[1, at, :] * east
                + coef[2, at, :] * west
                + coef[3, at, :] * north
                + coef[4, at, :] * south
            )

    def forecast(k):
        base = pl.multiple_of(k * 8, 8)
        advance(xt, k * 8, step_a, 0, 14, base, 5)
        advance(step_a, 0, step_b, 0, 12, base, 6)
        advance(step_b, 0, step_a, 0, 10, base, 7)
        advance(step_a, 0, fsend, k * 8, 8, base, 8)

    def send_rows(k, c, row, count, sem):
        remote(
            fsend.at[pl.ds(k * 8 + 4 * c + row, count)],
            fields.at[pl.ds(row, count), pl.ds(pl.multiple_of(g * MEM, MEM), MEM), :],
            fwd_send, sem, (s, 2 * k + c),
        ).start()

    def send_first(k, c):
        send_rows(k, c, 0, 1, fwd_recv.at[0])
        send_rows(k, c, TILE_ROWS - 1, 1, fwd_recv.at[0])

    def send_later(row, sem):
        def others(i, carry):
            k = target(i)
            for c in range(2):
                send_rows(k, c, row, 1, sem)
            return carry

        lax.fori_loop(1, CHIPS, others, 0)
        send_rows(chip, 1 - core, row, 1, sem)

    def first_rows(i, carry):
        @pl.when(i == 5)
        def _():
            for copy in halos:
                copy.wait()
            coefficients(0, jnp.where(s == 0, 0.0, 1.0).astype(F32))
            coefficients(ROWS + 8, jnp.where(s == SLABS - 1, 0.0, 1.0).astype(F32))

            @pl.when(s == 0)
            def _():
                xt[pl.ds(0, 4)] = jnp.zeros((4, MEM, LON), F32)

            @pl.when(s == SLABS - 1)
            def _():
                xt[pl.ds(ROWS + 4, 4)] = jnp.zeros((4, MEM, LON), F32)

        k = early_target(i)
        forecast(k)

        @pl.when(i == 1)
        def _():
            pl.semaphore_wait(barrier, GROUPS - 1 + 4)
            for copy in halos:
                copy.start()

        for c in range(2):
            send_first(k, c)
        return carry

    lax.fori_loop(1, CHIPS, first_rows, 0)
    forecast(chip)
    send_first(chip, 1 - core)
    own = pltpu.make_async_copy(
        fsend.at[pl.ds(g * 4, 4)], fields.at[:, pl.ds(pl.multiple_of(g * MEM, MEM), MEM), :], own_sem.at[0]
    )
    own.start()
    send_later(1, fwd_recv.at[1])

    load_i.wait()
    scale = 1.0 / ((R + 1.0) * (MEMBERS - 1.0))
    for row in range(TILE_ROWS):
        cols = pl.ds(row * ROW_OBS, ROW_OBS)
        wgt[row + 1] = inn[:, cols] * (prec_ref[:, cols] * scale)

    def split_weights(slot):
        wgt_high[slot], wgt_low[slot] = split(wgt[slot])

    def split_observed(slot):
        obs_high[slot], obs_low[slot] = split(obs[slot])

    def send_rim(array, src, dst, n, device):
        def piece(p, carry):
            part = pl.ds(pl.multiple_of(p * OB, OB), OB)
            remote(array.at[src, part], array.at[dst, part], rim_send.at[n], rim_recv.at[n], device).start()
            return carry

        lax.fori_loop(0, ROW_OBS // OB, piece, 0)

    def rim_wait(array, sem):
        pltpu.make_async_copy(array.at[0], array.at[0], sem).wait()

    send_rim(wgt, TILE_ROWS, 0, 0, nxt_id)
    send_rim(wgt, 1, TILE_ROWS + 1, 1, prv_id)

    for row in range(TILE_ROWS):
        split_weights(row + 1)

    square[...] = jnp.zeros_like(square)
    square[pl.ds(0, TILE_BLOCKS), pl.ds(0, OB)] = cell_ref[...].astype(F32)
    cells = square[...].T
    lane = lax.broadcasted_iota(jnp.int32, (OB, 128), 1).astype(F32)
    for b in range(TILE_BLOCKS):
        pick[b] = jnp.where(lane == cells[:OB, b : b + 1], 1.0, 0.0).astype(BF16)

    block = lax.broadcasted_iota(jnp.int32, (128, TILE_BLOCKS), 1)
    slot_row = lax.broadcasted_iota(jnp.int32, (128, TILE_BLOCKS), 0)
    here = flat * TILE_BLOCKS + block
    row_start = flat * TILE_BLOCKS + jnp.bitwise_and(block, -8) - R
    total = jnp.zeros((128, TILE_BLOCKS), F32)
    for n in range(R + 1):
        chosen = band_ref[n : n + 1, :]
        height = (R + 1.0) - jnp.abs(chosen - here).astype(F32)
        total = total + jnp.where(slot_row == chosen - row_start, height, 0.0)
    square[:, pl.ds(0, TILE_BLOCKS)] = total
    taper[...] = square[...].T[:TILE_BLOCKS]

    own.wait()

    def prepare(row):
        def columns(c, carry):
            cols = pl.ds(pl.multiple_of(c * 256, 256), 256)
            field = fields[row, :, cols]
            mean = jnp.sum(field, axis=0, keepdims=True) * (1.0 / MEMBERS)
            high, low = split(field - mean)
            anom_high[row, :, cols] = high
            anom_low[row, :, cols] = low
            for b in range(2):
                pair = pl.ds(pl.multiple_of(c * 64 + b * OB, OB), OB)
                chosen = pick[row * ROW_BLOCKS + c * 2 + b]
                part = slice(b * 128, b * 128 + 128)
                obs[row + 1, pair, :] = dot_t(chosen, high[:, part]) + dot_t(chosen, low[:, part])
            return carry

        lax.fori_loop(0, 4, columns, 0)
        split_observed(row + 1)

    def arrived(row, count, sem):
        view = fields.at[pl.ds(row, count), pl.ds(0, MEMBERS - MEM), :]
        pltpu.make_async_copy(view, view, sem).wait()

    def analyse(row):
        def columns(c, carry):
            cols = pl.ds(pl.multiple_of(c * 256, 256), 256)
            high = anom_high[row, :, cols]
            low = anom_low[row, :, cols]
            weights = [taper[pl.ds(row * ROW_BLOCKS + c * 2 + b, 1), :] for b in range(2)]
            total = fields[row, :, cols]
            for part in range(3):
                slot = row + part
                cross = dot3(obs_high[slot], obs_low[slot], high, low)
                spread = jnp.concatenate(
                    [
                        jnp.concatenate(
                            [
                                jnp.broadcast_to(weights[b][:, part * 8 + j : part * 8 + j + 1], (OB, 128))
                                for b in range(2)
                            ],
                            axis=1,
                        )
                        for j in range(8)
                    ],
                    axis=0,
                )
                cross_high, cross_low = split(cross * spread)
                total = total + dot3(wgt_high[slot], wgt_low[slot], cross_high, cross_low)
            upd[row, :, cols] = total
            return carry

        lax.fori_loop(0, 4, columns, 0)

    def give_back(row):
        def one(k, c):
            d = 2 * k + c
            remote(
                upd.at[row, pl.ds(pl.multiple_of(d * MEM, MEM), MEM), :], ret_ref.at[TILE_ROWS * g + row],
                ret_send, ret_recv, (s, d),
            ).start()

        def others(i, carry):
            k = target(i)
            for c in range(2):
                one(k, c)
            return carry

        lax.fori_loop(1, CHIPS, others, 0)
        one(chip, 1 - core)

    arrived(0, 2, fwd_recv.at[0])

    def prepare_edge(t, carry):
        prepare(t * (TILE_ROWS - 1))
        return carry

    lax.fori_loop(0, 2, prepare_edge, 0)
    send_rim(obs, TILE_ROWS, 0, 2, nxt_id)
    send_rim(obs, 1, TILE_ROWS + 1, 3, prv_id)
    send_later(2, fwd_recv.at[2])

    def finish(row, carry):
        @pl.when(row == 0)
        def _():
            arrived(1, 1, fwd_recv.at[1])

        @pl.when(row == 1)
        def _():
            arrived(2, 1, fwd_recv.at[2])

        @pl.when(row < 2)
        def _():
            prepare(row + 1)

        @pl.when(row == 0)
        def _():
            for n in range(2):
                rim_wait(wgt, rim_recv.at[n])
                rim_wait(obs, rim_recv.at[n + 2])
            for slot in (0, TILE_ROWS + 1):
                split_weights(slot)
                split_observed(slot)

        analyse(row)
        give_back(row)
        return carry

    lax.fori_loop(0, TILE_ROWS, finish, 0)

    keep = pltpu.make_async_copy(
        upd.at[:, pl.ds(pl.multiple_of(g * MEM, MEM), MEM), :], ret_ref.at[pl.ds(TILE_ROWS * g, TILE_ROWS)], own_sem.at[1]
    )
    keep.start()
    for n in range(4):
        rim_wait(wgt, rim_send.at[n])
    sent = fsend.at[pl.ds(0, ROWS - 4)]
    pltpu.make_async_copy(sent, sent, fwd_send).wait()
    keep.wait()
    back = ret_ref.at[pl.ds(0, ROWS - 4)]
    pltpu.make_async_copy(back, back, ret_send).wait()
    pltpu.make_async_copy(back, back, ret_recv).wait()


def turn_kernel(rows_ref, out_ref):
    out_ref[...] = jnp.swapaxes(rows_ref[...], 0, 1)


def shards(initial, stencil_numbers, innovations, obs_prec, obs_cell, band_idx):
    vmem = pl.BlockSpec(memory_space=pltpu.VMEM)
    hbm = pl.BlockSpec(memory_space=pl.ANY)
    dma = pltpu.SemaphoreType.DMA
    rows = pl.pallas_call(
        cycle_kernel,
        out_shape=jax.ShapeDtypeStruct((ROWS, MEM, LON), F32),
        in_specs=[hbm, hbm, hbm, vmem, vmem, vmem],
        out_specs=hbm,
        scratch_shapes=[
            pltpu.VMEM((MEM, ROWS, LON), F32),
            pltpu.VMEM((ROWS + 8, MEM, LON), F32),
            pltpu.VMEM((3, ROWS + 16, LON), F32),
            pltpu.VMEM((5, ROWS + 16, LON), F32),
            pltpu.VMEM((14, MEM, LON), F32),
            pltpu.VMEM((14, MEM, LON), F32),
            pltpu.VMEM((ROWS, MEM, LON), F32),
            pltpu.VMEM((TILE_ROWS, MEMBERS, LON), F32),
            pltpu.VMEM((TILE_ROWS, MEMBERS, LON), BF16),
            pltpu.VMEM((TILE_ROWS, MEMBERS, LON), BF16),
            pltpu.VMEM((TILE_BLOCKS, OB, 128), BF16),
            pltpu.VMEM((TILE_ROWS + 2, ROW_OBS, MEMBERS), F32),
            pltpu.VMEM((TILE_ROWS + 2, ROW_OBS, MEMBERS), BF16),
            pltpu.VMEM((TILE_ROWS + 2, ROW_OBS, MEMBERS), BF16),
            pltpu.VMEM((TILE_ROWS + 2, MEMBERS, ROW_OBS), F32),
            pltpu.VMEM((TILE_ROWS + 2, MEMBERS, ROW_OBS), BF16),
            pltpu.VMEM((TILE_ROWS + 2, MEMBERS, ROW_OBS), BF16),
            pltpu.VMEM((MEMBERS, TILE_ROWS * ROW_OBS), F32),
            pltpu.VMEM((128, 128), F32),
            pltpu.VMEM((TILE_BLOCKS, 128), F32),
            pltpu.VMEM((TILE_ROWS, MEMBERS, LON), F32),
            dma((3,)),
            dma((4,)),
            dma((4,)),
            dma(()),
            dma((3,)),
            dma((2,)),
            dma((4,)),
            dma((4,)),
            dma(()),
            dma(()),
        ],
        compiler_params=pltpu.CompilerParams(
            collective_id=0, has_side_effects=True, vmem_limit_bytes=60 * 2**20
        ),
        name="cycle",
    )(initial, stencil_numbers, innovations, obs_prec.reshape(1, -1), obs_cell, band_idx.T)
    group = 32
    return pl.pallas_call(
        turn_kernel,
        grid=(ROWS // group,),
        out_shape=jax.ShapeDtypeStruct((MEM, ROWS, LON), F32),
        in_specs=[pl.BlockSpec((group, MEM, LON), lambda i: (i, 0, 0))],
        out_specs=pl.BlockSpec((MEM, group, LON), lambda i: (0, i, 0)),
        compiler_params=pltpu.CompilerParams(vmem_limit_bytes=60 * 2**20),
        name="turn",
    )(rows)


def solution(mesh):
    in_specs = (
        P("member", "slab", None),
        P(None, "slab", None),
        P(None, ("slab", "member")),
        P(("slab", "member")),
        P(("slab", "member"), None),
        P(("slab", "member"), None),
    )
    out_specs = P("member", "slab", None)
    return jax.shard_map(shards, mesh=mesh, in_specs=in_specs, out_specs=out_specs, check_vma=False)
```

```python
import functools

import jax
import jax.numpy as jnp
from jax import lax
from jax.experimental import pallas as pl
from jax.experimental.pallas import tpu as pltpu
from jax.sharding import PartitionSpec as P

MESH = pl.DeviceIdType.MESH
F32 = jnp.float32
BF16 = jnp.bfloat16
OB = 32
R = 8
SLABS = 4
GROUPS = 32
CHIPS = 16
ROWS = 128
LON = 1024
MEM = 8
MEMBERS = 256
TILE_ROWS = 4
ROW_BLOCKS = 8
TILE_BLOCKS = 32
ROW_OBS = ROW_BLOCKS * OB
TURN_ROWS = 16


def split(value):
    high = value.astype(BF16)
    low = (value - high.astype(F32)).astype(BF16)
    return high, low


def dot3(a_high, a_low, b_high, b_low):
    dot = functools.partial(jnp.dot, preferred_element_type=F32)
    return dot(a_high, b_high) + dot(a_high, b_low) + dot(a_low, b_high)


def dot_t(a, b):
    return lax.dot_general(a, b, (((1,), (1,)), ((), ())), preferred_element_type=F32)


def cycle_kernel(
    init_ref, sten_ref, inn_ref, prec_ref, cell_ref, band_ref, ret_ref,
    xbuf, xt, sten, coef, step_a, step_b, fsend, fields, anom_high, anom_low,
    pick, obs, obs_high, obs_low, wgt, wgt_high, wgt_low, inn, square, taper, upd,
    load_sem, halo_send, halo_recv, fwd_send, fwd_recv, own_sem, rim_send, rim_recv, ret_send, ret_recv,
):
    s = lax.axis_index("slab")
    g = lax.axis_index("member")
    chip = g // 2
    core = g % 2
    flat = s * GROUPS + g
    up = lax.rem(s + 1, SLABS)
    down = lax.rem(s + SLABS - 1, SLABS)
    nxt = lax.rem(flat + 1, SLABS * GROUPS)
    prv = lax.rem(flat + SLABS * GROUPS - 1, SLABS * GROUPS)
    nxt_id = (nxt // GROUPS, lax.rem(nxt, GROUPS))
    prv_id = (prv // GROUPS, lax.rem(prv, GROUPS))

    barrier = pltpu.get_barrier_semaphore()

    def greet(i, carry):
        peer = lax.rem(g + i, GROUPS)
        pl.semaphore_signal(barrier, inc=1, device_id=(s, peer), device_id_type=MESH)
        return carry

    for device in ((up, g), (down, g), nxt_id, prv_id):
        pl.semaphore_signal(barrier, inc=1, device_id=device, device_id_type=MESH)
    lax.fori_loop(1, GROUPS, greet, 0)

    load_x = pltpu.make_async_copy(init_ref, xbuf, load_sem.at[0])
    load_s = pltpu.make_async_copy(sten_ref, sten.at[:, pl.ds(8, ROWS), :], load_sem.at[1])
    load_i = pltpu.make_async_copy(inn_ref, inn, load_sem.at[2])
    load_x.start()
    load_s.start()
    load_i.start()

    load_x.wait()

    def turn(k, carry):
        start = pl.multiple_of(k * 8, 8)
        rows = xbuf[:, pl.ds(start, 8), :]
        xt[pl.ds(k * 8 + 4, 8)] = jnp.swapaxes(rows, 0, 1)
        return carry

    lax.fori_loop(0, CHIPS, turn, 0)

    def coefficients(start, live):
        rows = pl.ds(start, 8)
        k = sten[0, rows, :] * live
        u = sten[1, rows, :] * (0.5 * live)
        v = sten[2, rows, :] * (0.5 * live)
        coef[0, rows, :] = 1.0 - 4.0 * k
        coef[1, rows, :] = k - u
        coef[2, rows, :] = k + u
        coef[3, rows, :] = k - v
        coef[4, rows, :] = k + v

    load_s.wait()

    def own_coefficients(t, carry):
        coefficients(pl.multiple_of(t * 8 + 8, 8), 1.0)
        return carry

    lax.fori_loop(0, CHIPS, own_coefficients, 0)

    def remote(src, dst, send_sem, recv_sem, device):
        return pltpu.make_async_remote_copy(
            src_ref=src, dst_ref=dst, send_sem=send_sem, recv_sem=recv_sem,
            device_id=device, device_id_type=MESH,
        )

    halos = [
        remote(sten_ref.at[:, pl.ds(ROWS - 8, 8), :], sten.at[:, pl.ds(0, 8), :], halo_send.at[0], halo_recv.at[0], (up, g)),
        remote(sten_ref.at[:, pl.ds(0, 8), :], sten.at[:, pl.ds(ROWS + 8, 8), :], halo_send.at[1], halo_recv.at[1], (down, g)),
        remote(xt.at[pl.ds(ROWS, 4)], xt.at[pl.ds(0, 4)], halo_send.at[2], halo_recv.at[2], (up, g)),
        remote(xt.at[pl.ds(4, 4)], xt.at[pl.ds(ROWS + 4, 4)], halo_send.at[3], halo_recv.at[3], (down, g)),
    ]

    def target(i):
        return lax.rem(chip + (7 + 2 * core) * i, CHIPS)

    def early_target(i):
        k = target(i)
        edge = 1 - (lax.rem(k + 1, CHIPS) + 14) // 16
        middle = 1 - (lax.rem(k + 9, CHIPS) + 14) // 16
        first = 1 - (i + 11) // 16
        later = ((i + 7) // 16) * (1 - (i + 3) // 16)
        return lax.rem(k + 8 * (first * edge + later * middle), CHIPS)

    def advance(src, src_start, dst, dst_start, count, coef_base, coef_offset):
        for row in range(count):
            centre = src[src_start + row + 1]
            north = src[src_start + row + 2]
            south = src[src_start + row]
            east = pltpu.roll(centre, LON - 1, 1)
            west = pltpu.roll(centre, 1, 1)
            at = pl.ds(coef_base + coef_offset + row, 1)
            dst[dst_start + row] = (
                coef[0, at, :] * centre
                + coef[1, at, :] * east
                + coef[2, at, :] * west
                + coef[3, at, :] * north
                + coef[4, at, :] * south
            )

    def forecast(k):
        base = pl.multiple_of(k * 8, 8)
        advance(xt, k * 8, step_a, 0, 14, base, 5)
        advance(step_a, 0, step_b, 0, 12, base, 6)
        advance(step_b, 0, step_a, 0, 10, base, 7)
        advance(step_a, 0, fsend, k * 8, 8, base, 8)

    def send_rows(k, c, row, count, sem):
        remote(
            fsend.at[pl.ds(k * 8 + 4 * c + row, count)],
            fields.at[pl.ds(row, count), pl.ds(pl.multiple_of(g * MEM, MEM), MEM), :],
            fwd_send, sem, (s, 2 * k + c),
        ).start()

    def send_first(k, c):
        send_rows(k, c, 0, 1, fwd_recv.at[0])
        send_rows(k, c, TILE_ROWS - 1, 1, fwd_recv.at[0])

    def send_later(row, sem):
        def others(i, carry):
            k = target(i)
            for c in range(2):
                send_rows(k, c, row, 1, sem)
            return carry

        lax.fori_loop(1, CHIPS, others, 0)
        send_rows(chip, 1 - core, row, 1, sem)

    def first_rows(i, carry):
        @pl.when(i == 5)
        def _():
            for copy in halos:
                copy.wait()
            coefficients(0, jnp.where(s == 0, 0.0, 1.0).astype(F32))
            coefficients(ROWS + 8, jnp.where(s == SLABS - 1, 0.0, 1.0).astype(F32))

            @pl.when(s == 0)
            def _():
                xt[pl.ds(0, 4)] = jnp.zeros((4, MEM, LON), F32)

            @pl.when(s == SLABS - 1)
            def _():
                xt[pl.ds(ROWS + 4, 4)] = jnp.zeros((4, MEM, LON), F32)

        k = early_target(i)
        forecast(k)

        @pl.when(i == 1)
        def _():
            pl.semaphore_wait(barrier, GROUPS - 1 + 4)
            for copy in halos:
                copy.start()

        for c in range(2):
            send_first(k, c)
        return carry

    lax.fori_loop(1, CHIPS, first_rows, 0)
    forecast(chip)
    send_first(chip, 1 - core)
    own = pltpu.make_async_copy(
        fsend.at[pl.ds(g * 4, 4)], fields.at[:, pl.ds(pl.multiple_of(g * MEM, MEM), MEM), :], own_sem.at[0]
    )
    own.start()
    send_later(1, fwd_recv.at[1])
    send_later(2, fwd_recv.at[2])

    load_i.wait()
    scale = 1.0 / ((R + 1.0) * (MEMBERS - 1.0))
    for row in range(TILE_ROWS):
        cols = pl.ds(row * ROW_OBS, ROW_OBS)
        wgt[row + 1] = inn[:, cols] * (prec_ref[:, cols] * scale)

    def split_weights(slot):
        wgt_high[slot], wgt_low[slot] = split(wgt[slot])

    def split_observed(slot):
        obs_high[slot], obs_low[slot] = split(obs[slot])

    def send_rim(array, src, dst, n, device):
        def piece(p, carry):
            part = pl.ds(pl.multiple_of(p * OB, OB), OB)
            remote(array.at[src, part], array.at[dst, part], rim_send.at[n], rim_recv.at[n], device).start()
            return carry

        lax.fori_loop(0, ROW_OBS // OB, piece, 0)

    def rim_wait(array, sem):
        pltpu.make_async_copy(array.at[0], array.at[0], sem).wait()


    for row in range(TILE_ROWS):
        split_weights(row + 1)

    square[...] = jnp.zeros_like(square)
    square[pl.ds(0, TILE_BLOCKS), pl.ds(0, OB)] = cell_ref[...].astype(F32)
    cells = square[...].T
    lane = lax.broadcasted_iota(jnp.int32, (OB, 128), 1).astype(F32)
    for b in range(TILE_BLOCKS):
        pick[b] = jnp.where(lane == cells[:OB, b : b + 1], 1.0, 0.0).astype(BF16)

    block = lax.broadcasted_iota(jnp.int32, (128, TILE_BLOCKS), 1)
    slot_row = lax.broadcasted_iota(jnp.int32, (128, TILE_BLOCKS), 0)
    here = flat * TILE_BLOCKS + block
    row_start = flat * TILE_BLOCKS + jnp.bitwise_and(block, -8) - R
    total = jnp.zeros((128, TILE_BLOCKS), F32)
    for n in range(R + 1):
        chosen = band_ref[n : n + 1, :]
        height = (R + 1.0) - jnp.abs(chosen - here).astype(F32)
        total = total + jnp.where(slot_row == chosen - row_start, height, 0.0)
    square[:, pl.ds(0, TILE_BLOCKS)] = total
    taper[...] = square[...].T[:TILE_BLOCKS]

    own.wait()

    def prepare(row):
        def columns(c, carry):
            cols = pl.ds(pl.multiple_of(c * 256, 256), 256)
            field = fields[row, :, cols]
            mean = jnp.sum(field, axis=0, keepdims=True) * (1.0 / MEMBERS)
            high, low = split(field - mean)
            anom_high[row, :, cols] = high
            anom_low[row, :, cols] = low
            for b in range(2):
                pair = pl.ds(pl.multiple_of(c * 64 + b * OB, OB), OB)
                chosen = pick[row * ROW_BLOCKS + c * 2 + b]
                part = slice(b * 128, b * 128 + 128)
                obs[row + 1, pair, :] = dot_t(chosen, high[:, part]) + dot_t(chosen, low[:, part])
            return carry

        lax.fori_loop(0, 4, columns, 0)
        split_observed(row + 1)

    def arrived(row, count, sem):
        view = fields.at[pl.ds(row, count), pl.ds(0, MEMBERS - MEM), :]
        pltpu.make_async_copy(view, view, sem).wait()

    def analyse(row, parts=(0, 1, 2), begun=False):
        def columns(c, carry):
            cols = pl.ds(pl.multiple_of(c * 256, 256), 256)
            high = anom_high[row, :, cols]
            low = anom_low[row, :, cols]
            weights = [taper[pl.ds(row * ROW_BLOCKS + c * 2 + b, 1), :] for b in range(2)]
            total = (upd if begun else fields)[row, :, cols]
            for part in parts:
                slot = row + part
                cross = dot3(obs_high[slot], obs_low[slot], high, low)
                spread = jnp.concatenate(
                    [
                        jnp.concatenate(
                            [
                                jnp.broadcast_to(weights[b][:, part * 8 + j : part * 8 + j + 1], (OB, 128))
                                for b in range(2)
                            ],
                            axis=1,
                        )
                        for j in range(8)
                    ],
                    axis=0,
                )
                cross_high, cross_low = split(cross * spread)
                total = total + dot3(wgt_high[slot], wgt_low[slot], cross_high, cross_low)
            upd[row, :, cols] = total
            return carry

        lax.fori_loop(0, 4, columns, 0)

    def give_back(row):
        def one(k, c):
            d = 2 * k + c
            remote(
                upd.at[row, pl.ds(pl.multiple_of(d * MEM, MEM), MEM), :], ret_ref.at[TILE_ROWS * g + row],
                ret_send, ret_recv, (s, d),
            ).start()

        def others(i, carry):
            k = target(i)
            for c in range(2):
                one(k, c)
            return carry

        lax.fori_loop(1, CHIPS, others, 0)
        one(chip, 1 - core)

    arrived(0, 2, fwd_recv.at[0])

    def prepare_first(t, carry):
        @pl.when(t == 2)
        def _():
            arrived(1, 1, fwd_recv.at[1])

        prepare(jnp.where(t == 1, TILE_ROWS - 1, t // 2))
        return carry

    lax.fori_loop(0, 3, prepare_first, 0)
    analyse(1, (0, 1))

    arrived(2, 1, fwd_recv.at[2])
    for array, n in ((obs, 2), (wgt, 0)):
        send_rim(array, TILE_ROWS, 0, n, nxt_id)
        send_rim(array, 1, TILE_ROWS + 1, n + 1, prv_id)
    prepare(2)
    analyse(1, (2,), begun=True)
    give_back(1)

    def finish(t, carry):
        @pl.when(t == 1)
        def _():
            for n in range(2):
                rim_wait(wgt, rim_recv.at[n])
                rim_wait(obs, rim_recv.at[n + 2])
            for slot in (0, TILE_ROWS + 1):
                split_weights(slot)
                split_observed(slot)

        row = jnp.where(t == 0, 2, (t - 1) * (TILE_ROWS - 1))
        analyse(row)
        give_back(row)
        return carry

    lax.fori_loop(0, 3, finish, 0)

    keep = pltpu.make_async_copy(
        upd.at[:, pl.ds(pl.multiple_of(g * MEM, MEM), MEM), :], ret_ref.at[pl.ds(TILE_ROWS * g, TILE_ROWS)], own_sem.at[1]
    )
    keep.start()
    for n in range(4):
        rim_wait(wgt, rim_send.at[n])
    sent = fsend.at[pl.ds(0, ROWS - 4)]
    pltpu.make_async_copy(sent, sent, fwd_send).wait()
    keep.wait()
    back = ret_ref.at[pl.ds(0, ROWS - 4)]
    pltpu.make_async_copy(back, back, ret_send).wait()
    pltpu.make_async_copy(back, back, ret_recv).wait()


def turn_kernel(rows_ref, out_ref, rows, turned, load_sem, store_sem):
    def load(n):
        part = pl.ds(n * TURN_ROWS, TURN_ROWS)
        return pltpu.make_async_copy(rows_ref.at[part], rows.at[part], load_sem.at[n])

    def store(n):
        part = pl.ds(n * TURN_ROWS, TURN_ROWS)
        return pltpu.make_async_copy(turned.at[:, part, :], out_ref.at[:, part, :], store_sem.at[n])

    count = ROWS // TURN_ROWS
    for n in range(count):
        load(n).start()
    for n in range(count):
        load(n).wait()
        for start in range(n * TURN_ROWS, (n + 1) * TURN_ROWS, 8):
            turned[:, pl.ds(start, 8), :] = jnp.swapaxes(rows[pl.ds(start, 8)], 0, 1)
        store(n).start()
    for n in range(count):
        store(n).wait()


def shards(initial, stencil_numbers, innovations, obs_prec, obs_cell, band_idx):
    vmem = pl.BlockSpec(memory_space=pltpu.VMEM)
    hbm = pl.BlockSpec(memory_space=pl.ANY)
    dma = pltpu.SemaphoreType.DMA
    rows = pl.pallas_call(
        cycle_kernel,
        out_shape=jax.ShapeDtypeStruct((ROWS, MEM, LON), F32),
        in_specs=[hbm, hbm, hbm, vmem, vmem, vmem],
        out_specs=hbm,
        scratch_shapes=[
            pltpu.VMEM((MEM, ROWS, LON), F32),
            pltpu.VMEM((ROWS + 8, MEM, LON), F32),
            pltpu.VMEM((3, ROWS + 16, LON), F32),
            pltpu.VMEM((5, ROWS + 16, LON), F32),
            pltpu.VMEM((14, MEM, LON), F32),
            pltpu.VMEM((14, MEM, LON), F32),
            pltpu.VMEM((ROWS, MEM, LON), F32),
            pltpu.VMEM((TILE_ROWS, MEMBERS, LON), F32),
            pltpu.VMEM((TILE_ROWS, MEMBERS, LON), BF16),
            pltpu.VMEM((TILE_ROWS, MEMBERS, LON), BF16),
            pltpu.VMEM((TILE_BLOCKS, OB, 128), BF16),
            pltpu.VMEM((TILE_ROWS + 2, ROW_OBS, MEMBERS), F32),
            pltpu.VMEM((TILE_ROWS + 2, ROW_OBS, MEMBERS), BF16),
            pltpu.VMEM((TILE_ROWS + 2, ROW_OBS, MEMBERS), BF16),
            pltpu.VMEM((TILE_ROWS + 2, MEMBERS, ROW_OBS), F32),
            pltpu.VMEM((TILE_ROWS + 2, MEMBERS, ROW_OBS), BF16),
            pltpu.VMEM((TILE_ROWS + 2, MEMBERS, ROW_OBS), BF16),
            pltpu.VMEM((MEMBERS, TILE_ROWS * ROW_OBS), F32),
            pltpu.VMEM((128, 128), F32),
            pltpu.VMEM((TILE_BLOCKS, 128), F32),
            pltpu.VMEM((TILE_ROWS, MEMBERS, LON), F32),
            dma((3,)),
            dma((4,)),
            dma((4,)),
            dma(()),
            dma((3,)),
            dma((2,)),
            dma((4,)),
            dma((4,)),
            dma(()),
            dma(()),
        ],
        compiler_params=pltpu.CompilerParams(
            collective_id=0, has_side_effects=True, vmem_limit_bytes=60 * 2**20
        ),
        name="cycle",
    )(initial, stencil_numbers, innovations, obs_prec.reshape(1, -1), obs_cell, band_idx.T)
    return pl.pallas_call(
        turn_kernel,
        out_shape=jax.ShapeDtypeStruct((MEM, ROWS, LON), F32),
        in_specs=[hbm],
        out_specs=hbm,
        scratch_shapes=[
            pltpu.VMEM((ROWS, MEM, LON), F32),
            pltpu.VMEM((MEM, ROWS, LON), F32),
            dma((ROWS // TURN_ROWS,)),
            dma((ROWS // TURN_ROWS,)),
        ],
        compiler_params=pltpu.CompilerParams(vmem_limit_bytes=60 * 2**20),
        name="turn",
    )(rows)


def solution(mesh):
    in_specs = (
        P("member", "slab", None),
        P(None, "slab", None),
        P(None, ("slab", "member")),
        P(("slab", "member")),
        P(("slab", "member"), None),
        P(("slab", "member"), None),
    )
    out_specs = P("member", "slab", None)
    return jax.shard_map(shards, mesh=mesh, in_specs=in_specs, out_specs=out_specs, check_vma=False)
```

```python
import functools

import jax
import jax.numpy as jnp
from jax import lax
from jax.experimental import pallas as pl
from jax.experimental.pallas import tpu as pltpu
from jax.sharding import PartitionSpec as P

MESH = pl.DeviceIdType.MESH
F32 = jnp.float32
BF16 = jnp.bfloat16
OB = 32
R = 8
SLABS = 4
GROUPS = 32
CHIPS = 16
ROWS = 128
LON = 1024
MEM = 8
MEMBERS = 256
TILE_ROWS = 4
ROW_BLOCKS = 8
TILE_BLOCKS = 32
ROW_OBS = ROW_BLOCKS * OB
TURN_ROWS = 16


def split(value):
    high = value.astype(BF16)
    low = (value - high.astype(F32)).astype(BF16)
    return high, low


def dot3(a_high, a_low, b_high, b_low):
    dot = functools.partial(jnp.dot, preferred_element_type=F32)
    return dot(a_high, b_high) + dot(a_high, b_low) + dot(a_low, b_high)


def dot_t(a, b):
    return lax.dot_general(a, b, (((1,), (1,)), ((), ())), preferred_element_type=F32)


def cycle_kernel(
    init_ref, sten_ref, inn_ref, prec_ref, cell_ref, band_ref, ret_ref,
    xbuf, xt, sten, coef, step_a, step_b, fsend, fields, anom_high, anom_low,
    pick, obs, obs_high, obs_low, wgt, wgt_high, wgt_low, inn, square, taper, upd,
    load_sem, halo_send, halo_recv, fwd_send, fwd_recv, own_sem, rim_send, rim_recv, ret_send, ret_recv,
):
    s = lax.axis_index("slab")
    g = lax.axis_index("member")
    chip = g // 2
    core = g % 2
    flat = s * GROUPS + g
    up = lax.rem(s + 1, SLABS)
    down = lax.rem(s + SLABS - 1, SLABS)
    nxt = lax.rem(flat + 1, SLABS * GROUPS)
    prv = lax.rem(flat + SLABS * GROUPS - 1, SLABS * GROUPS)
    nxt_id = (nxt // GROUPS, lax.rem(nxt, GROUPS))
    prv_id = (prv // GROUPS, lax.rem(prv, GROUPS))

    barrier = pltpu.get_barrier_semaphore()

    def greet(i, carry):
        peer = lax.rem(g + i, GROUPS)
        pl.semaphore_signal(barrier, inc=1, device_id=(s, peer), device_id_type=MESH)
        return carry

    for device in ((up, g), (down, g), nxt_id, prv_id):
        pl.semaphore_signal(barrier, inc=1, device_id=device, device_id_type=MESH)
    lax.fori_loop(1, GROUPS, greet, 0)

    load_x = pltpu.make_async_copy(init_ref, xbuf, load_sem.at[0])
    load_s = pltpu.make_async_copy(sten_ref, sten.at[:, pl.ds(8, ROWS), :], load_sem.at[1])
    load_i = pltpu.make_async_copy(inn_ref, inn, load_sem.at[2])
    load_x.start()
    load_s.start()
    load_i.start()

    load_x.wait()

    def turn(k, carry):
        start = pl.multiple_of(k * 8, 8)
        rows = xbuf[:, pl.ds(start, 8), :]
        xt[pl.ds(k * 8 + 4, 8)] = jnp.swapaxes(rows, 0, 1)
        return carry

    lax.fori_loop(0, CHIPS, turn, 0)

    def coefficients(start, live):
        rows = pl.ds(start, 8)
        k = sten[0, rows, :] * live
        u = sten[1, rows, :] * (0.5 * live)
        v = sten[2, rows, :] * (0.5 * live)
        coef[0, rows, :] = 1.0 - 4.0 * k
        coef[1, rows, :] = k - u
        coef[2, rows, :] = k + u
        coef[3, rows, :] = k - v
        coef[4, rows, :] = k + v

    load_s.wait()

    def own_coefficients(t, carry):
        coefficients(pl.multiple_of(t * 8 + 8, 8), 1.0)
        return carry

    lax.fori_loop(0, CHIPS, own_coefficients, 0)

    def remote(src, dst, send_sem, recv_sem, device):
        return pltpu.make_async_remote_copy(
            src_ref=src, dst_ref=dst, send_sem=send_sem, recv_sem=recv_sem,
            device_id=device, device_id_type=MESH,
        )

    halos = [
        remote(sten_ref.at[:, pl.ds(ROWS - 8, 8), :], sten.at[:, pl.ds(0, 8), :], halo_send.at[0], halo_recv.at[0], (up, g)),
        remote(sten_ref.at[:, pl.ds(0, 8), :], sten.at[:, pl.ds(ROWS + 8, 8), :], halo_send.at[1], halo_recv.at[1], (down, g)),
        remote(xt.at[pl.ds(ROWS, 4)], xt.at[pl.ds(0, 4)], halo_send.at[2], halo_recv.at[2], (up, g)),
        remote(xt.at[pl.ds(4, 4)], xt.at[pl.ds(ROWS + 4, 4)], halo_send.at[3], halo_recv.at[3], (down, g)),
    ]

    def target(i):
        return lax.rem(chip + (7 + 2 * core) * i, CHIPS)

    def advance(src, src_start, dst, dst_start, count, coef_base, coef_offset):
        for row in range(count):
            centre = src[src_start + row + 1]
            north = src[src_start + row + 2]
            south = src[src_start + row]
            east = pltpu.roll(centre, LON - 1, 1)
            west = pltpu.roll(centre, 1, 1)
            at = pl.ds(coef_base + coef_offset + row, 1)
            dst[dst_start + row] = (
                coef[0, at, :] * centre
                + coef[1, at, :] * east
                + coef[2, at, :] * west
                + coef[3, at, :] * north
                + coef[4, at, :] * south
            )

    def forecast(k):
        base = pl.multiple_of(k * 8, 8)
        advance(xt, k * 8, step_a, 0, 14, base, 5)
        advance(step_a, 0, step_b, 0, 12, base, 6)
        advance(step_b, 0, step_a, 0, 10, base, 7)
        advance(step_a, 0, fsend, k * 8, 8, base, 8)

    def send_rows(k, c, row, count, sem):
        remote(
            fsend.at[pl.ds(k * 8 + 4 * c + row, count)],
            fields.at[pl.ds(row, count), pl.ds(pl.multiple_of(g * MEM, MEM), MEM), :],
            fwd_send, sem, (s, 2 * k + c),
        ).start()

    def half(t):
        row = t * TILE_ROWS
        advance(xt, row, step_a, 0, 10, row, 5)
        advance(step_a, 0, step_b, 0, 8, row, 6)
        advance(step_b, 0, step_a, 0, 6, row, 7)
        advance(step_a, 0, fsend, row, 4, row, 8)

    def send_row(k, c, row):
        send_rows(k, c, row, 1, fwd_recv.at[{0: 0, 3: 0, 1: 1, 2: 2}[row]])

    def is_inner(k):
        return (k > 0) & (k < CHIPS - 1)

    def first_rows(i, carry):
        k = target(i)
        inner = is_inner(k)

        @pl.when(inner)
        def _():
            forecast(k)

        @pl.when(k == 0)
        def _():
            half(1)

        @pl.when(k == CHIPS - 1)
        def _():
            half(GROUPS - 2)

        @pl.when(i == 1)
        def _():
            pl.semaphore_wait(barrier, GROUPS - 1 + 4)
            for copy in halos:
                copy.start()

        @pl.when(inner)
        def _():
            for c in range(2):
                send_row(k, c, 0)
                send_row(k, c, 3)

        @pl.when(jnp.logical_not(inner))
        def _():
            for row in (0, 3, 1, 2):
                send_row(k, 1 - k // (CHIPS - 1), row)

        return carry

    lax.fori_loop(1, CHIPS, first_rows, 0)

    for copy in halos:
        copy.wait()
    coefficients(0, jnp.where(s == 0, 0.0, 1.0).astype(F32))
    coefficients(ROWS + 8, jnp.where(s == SLABS - 1, 0.0, 1.0).astype(F32))

    @pl.when(s == 0)
    def _():
        xt[pl.ds(0, 4)] = jnp.zeros((4, MEM, LON), F32)

    @pl.when(s == SLABS - 1)
    def _():
        xt[pl.ds(ROWS + 4, 4)] = jnp.zeros((4, MEM, LON), F32)

    half(0)
    half(GROUPS - 1)

    @pl.when(is_inner(chip))
    def _():
        forecast(chip)

    @pl.when(chip == 0)
    def _():
        half(1)

    @pl.when(chip == CHIPS - 1)
    def _():
        half(GROUPS - 2)

    for row in (0, 3):
        send_row(chip, 1 - core, row)
    own = pltpu.make_async_copy(
        fsend.at[pl.ds(g * 4, 4)], fields.at[:, pl.ds(pl.multiple_of(g * MEM, MEM), MEM), :], own_sem.at[0]
    )
    own.start()

    for row, border_rows in ((1, (0, 3)), (2, (1, 2))):
        def others(i, carry, row=row, border_rows=border_rows):
            k = target(i)

            @pl.when(is_inner(k))
            def _():
                for c in range(2):
                    send_row(k, c, row)

            @pl.when(jnp.logical_not(is_inner(k)))
            def _():
                for border_row in border_rows:
                    send_row(k, k // (CHIPS - 1), border_row)

            return carry

        lax.fori_loop(1, CHIPS, others, 0)
        send_row(chip, 1 - core, row)

    load_i.wait()
    scale = 1.0 / ((R + 1.0) * (MEMBERS - 1.0))
    for row in range(TILE_ROWS):
        cols = pl.ds(row * ROW_OBS, ROW_OBS)
        wgt[row + 1] = inn[:, cols] * (prec_ref[:, cols] * scale)

    def split_weights(slot):
        wgt_high[slot], wgt_low[slot] = split(wgt[slot])

    def split_observed(slot):
        obs_high[slot], obs_low[slot] = split(obs[slot])

    def send_rim(array, src, dst, n, device):
        def piece(p, carry):
            part = pl.ds(pl.multiple_of(p * OB, OB), OB)
            remote(array.at[src, part], array.at[dst, part], rim_send.at[n], rim_recv.at[n], device).start()
            return carry

        lax.fori_loop(0, ROW_OBS // OB, piece, 0)

    def rim_wait(array, sem):
        pltpu.make_async_copy(array.at[0], array.at[0], sem).wait()


    for row in range(TILE_ROWS):
        split_weights(row + 1)

    square[...] = jnp.zeros_like(square)
    square[pl.ds(0, TILE_BLOCKS), pl.ds(0, OB)] = cell_ref[...].astype(F32)
    cells = square[...].T
    lane = lax.broadcasted_iota(jnp.int32, (OB, 128), 1).astype(F32)
    for b in range(TILE_BLOCKS):
        pick[b] = jnp.where(lane == cells[:OB, b : b + 1], 1.0, 0.0).astype(BF16)

    block = lax.broadcasted_iota(jnp.int32, (128, TILE_BLOCKS), 1)
    slot_row = lax.broadcasted_iota(jnp.int32, (128, TILE_BLOCKS), 0)
    here = flat * TILE_BLOCKS + block
    row_start = flat * TILE_BLOCKS + jnp.bitwise_and(block, -8) - R
    total = jnp.zeros((128, TILE_BLOCKS), F32)
    for n in range(R + 1):
        chosen = band_ref[n : n + 1, :]
        height = (R + 1.0) - jnp.abs(chosen - here).astype(F32)
        total = total + jnp.where(slot_row == chosen - row_start, height, 0.0)
    square[:, pl.ds(0, TILE_BLOCKS)] = total
    taper[...] = square[...].T[:TILE_BLOCKS]

    own.wait()

    def prepare(row):
        def columns(c, carry):
            cols = pl.ds(pl.multiple_of(c * 256, 256), 256)
            field = fields[row, :, cols]
            mean = jnp.sum(field, axis=0, keepdims=True) * (1.0 / MEMBERS)
            high, low = split(field - mean)
            anom_high[row, :, cols] = high
            anom_low[row, :, cols] = low
            for b in range(2):
                pair = pl.ds(pl.multiple_of(c * 64 + b * OB, OB), OB)
                chosen = pick[row * ROW_BLOCKS + c * 2 + b]
                part = slice(b * 128, b * 128 + 128)
                obs[row + 1, pair, :] = dot_t(chosen, high[:, part]) + dot_t(chosen, low[:, part])
            return carry

        lax.fori_loop(0, 4, columns, 0)
        split_observed(row + 1)

    def arrived(row, count, sem):
        view = fields.at[pl.ds(row, count), pl.ds(0, MEMBERS - MEM), :]
        pltpu.make_async_copy(view, view, sem).wait()

    def analyse(row, parts=(0, 1, 2), begun=False):
        def columns(c, carry):
            cols = pl.ds(pl.multiple_of(c * 256, 256), 256)
            high = anom_high[row, :, cols]
            low = anom_low[row, :, cols]
            weights = [taper[pl.ds(row * ROW_BLOCKS + c * 2 + b, 1), :] for b in range(2)]
            total = (upd if begun else fields)[row, :, cols]
            for part in parts:
                slot = row + part
                cross = dot3(obs_high[slot], obs_low[slot], high, low)
                spread = jnp.concatenate(
                    [
                        jnp.concatenate(
                            [
                                jnp.broadcast_to(weights[b][:, part * 8 + j : part * 8 + j + 1], (OB, 128))
                                for b in range(2)
                            ],
                            axis=1,
                        )
                        for j in range(8)
                    ],
                    axis=0,
                )
                cross_high, cross_low = split(cross * spread)
                total = total + dot3(wgt_high[slot], wgt_low[slot], cross_high, cross_low)
            upd[row, :, cols] = total
            return carry

        lax.fori_loop(0, 4, columns, 0)

    def give_back(row):
        def one(k, c):
            d = 2 * k + c
            remote(
                upd.at[row, pl.ds(pl.multiple_of(d * MEM, MEM), MEM), :], ret_ref.at[TILE_ROWS * g + row],
                ret_send, ret_recv, (s, d),
            ).start()

        def others(i, carry):
            k = target(i)
            for c in range(2):
                one(k, c)
            return carry

        lax.fori_loop(1, CHIPS, others, 0)
        one(chip, 1 - core)

    arrived(0, 2, fwd_recv.at[0])

    def prepare_first(t, carry):
        @pl.when(t == 2)
        def _():
            arrived(1, 1, fwd_recv.at[1])

        prepare(jnp.where(t == 1, TILE_ROWS - 1, t // 2))
        return carry

    lax.fori_loop(0, 3, prepare_first, 0)
    analyse(1, (0, 1))

    arrived(2, 1, fwd_recv.at[2])
    for array, n in ((obs, 2), (wgt, 0)):
        send_rim(array, TILE_ROWS, 0, n, nxt_id)
        send_rim(array, 1, TILE_ROWS + 1, n + 1, prv_id)
    prepare(2)
    analyse(1, (2,), begun=True)
    give_back(1)

    def finish(t, carry):
        @pl.when(t == 1)
        def _():
            for n in range(2):
                rim_wait(wgt, rim_recv.at[n])
                rim_wait(obs, rim_recv.at[n + 2])
            for slot in (0, TILE_ROWS + 1):
                split_weights(slot)
                split_observed(slot)

        row = jnp.where(t == 0, 2, (t - 1) * (TILE_ROWS - 1))
        analyse(row)
        give_back(row)
        return carry

    lax.fori_loop(0, 3, finish, 0)

    keep = pltpu.make_async_copy(
        upd.at[:, pl.ds(pl.multiple_of(g * MEM, MEM), MEM), :], ret_ref.at[pl.ds(TILE_ROWS * g, TILE_ROWS)], own_sem.at[1]
    )
    keep.start()
    for n in range(4):
        rim_wait(wgt, rim_send.at[n])
    sent = fsend.at[pl.ds(0, ROWS - 4)]
    pltpu.make_async_copy(sent, sent, fwd_send).wait()
    keep.wait()
    back = ret_ref.at[pl.ds(0, ROWS - 4)]
    pltpu.make_async_copy(back, back, ret_send).wait()
    pltpu.make_async_copy(back, back, ret_recv).wait()


def turn_kernel(rows_ref, out_ref, rows, turned, load_sem, store_sem):
    def load(n):
        part = pl.ds(n * TURN_ROWS, TURN_ROWS)
        return pltpu.make_async_copy(rows_ref.at[part], rows.at[part], load_sem.at[n])

    def store(n):
        part = pl.ds(n * TURN_ROWS, TURN_ROWS)
        return pltpu.make_async_copy(turned.at[:, part, :], out_ref.at[:, part, :], store_sem.at[n])

    count = ROWS // TURN_ROWS
    for n in range(count):
        load(n).start()
    for n in range(count):
        load(n).wait()
        for start in range(n * TURN_ROWS, (n + 1) * TURN_ROWS, 8):
            turned[:, pl.ds(start, 8), :] = jnp.swapaxes(rows[pl.ds(start, 8)], 0, 1)
        store(n).start()
    for n in range(count):
        store(n).wait()


def shards(initial, stencil_numbers, innovations, obs_prec, obs_cell, band_idx):
    vmem = pl.BlockSpec(memory_space=pltpu.VMEM)
    hbm = pl.BlockSpec(memory_space=pl.ANY)
    dma = pltpu.SemaphoreType.DMA
    rows = pl.pallas_call(
        cycle_kernel,
        out_shape=jax.ShapeDtypeStruct((ROWS, MEM, LON), F32),
        in_specs=[hbm, hbm, hbm, vmem, vmem, vmem],
        out_specs=hbm,
        scratch_shapes=[
            pltpu.VMEM((MEM, ROWS, LON), F32),
            pltpu.VMEM((ROWS + 8, MEM, LON), F32),
            pltpu.VMEM((3, ROWS + 16, LON), F32),
            pltpu.VMEM((5, ROWS + 16, LON), F32),
            pltpu.VMEM((14, MEM, LON), F32),
            pltpu.VMEM((14, MEM, LON), F32),
            pltpu.VMEM((ROWS, MEM, LON), F32),
            pltpu.VMEM((TILE_ROWS, MEMBERS, LON), F32),
            pltpu.VMEM((TILE_ROWS, MEMBERS, LON), BF16),
            pltpu.VMEM((TILE_ROWS, MEMBERS, LON), BF16),
            pltpu.VMEM((TILE_BLOCKS, OB, 128), BF16),
            pltpu.VMEM((TILE_ROWS + 2, ROW_OBS, MEMBERS), F32),
            pltpu.VMEM((TILE_ROWS + 2, ROW_OBS, MEMBERS), BF16),
            pltpu.VMEM((TILE_ROWS + 2, ROW_OBS, MEMBERS), BF16),
            pltpu.VMEM((TILE_ROWS + 2, MEMBERS, ROW_OBS), F32),
            pltpu.VMEM((TILE_ROWS + 2, MEMBERS, ROW_OBS), BF16),
            pltpu.VMEM((TILE_ROWS + 2, MEMBERS, ROW_OBS), BF16),
            pltpu.VMEM((MEMBERS, TILE_ROWS * ROW_OBS), F32),
            pltpu.VMEM((128, 128), F32),
            pltpu.VMEM((TILE_BLOCKS, 128), F32),
            pltpu.VMEM((TILE_ROWS, MEMBERS, LON), F32),
            dma((3,)),
            dma((4,)),
            dma((4,)),
            dma(()),
            dma((3,)),
            dma((2,)),
            dma((4,)),
            dma((4,)),
            dma(()),
            dma(()),
        ],
        compiler_params=pltpu.CompilerParams(
            collective_id=0, has_side_effects=True, vmem_limit_bytes=60 * 2**20
        ),
        name="cycle",
    )(initial, stencil_numbers, innovations, obs_prec.reshape(1, -1), obs_cell, band_idx.T)
    return pl.pallas_call(
        turn_kernel,
        out_shape=jax.ShapeDtypeStruct((MEM, ROWS, LON), F32),
        in_specs=[hbm],
        out_specs=hbm,
        scratch_shapes=[
            pltpu.VMEM((ROWS, MEM, LON), F32),
            pltpu.VMEM((MEM, ROWS, LON), F32),
            dma((ROWS // TURN_ROWS,)),
            dma((ROWS // TURN_ROWS,)),
        ],
        compiler_params=pltpu.CompilerParams(vmem_limit_bytes=60 * 2**20),
        name="turn",
    )(rows)


def solution(mesh):
    in_specs = (
        P("member", "slab", None),
        P(None, "slab", None),
        P(None, ("slab", "member")),
        P(("slab", "member")),
        P(("slab", "member"), None),
        P(("slab", "member"), None),
    )
    out_specs = P("member", "slab", None)
    return jax.shard_map(shards, mesh=mesh, in_specs=in_specs, out_specs=out_specs, check_vma=False)
```

```python
import functools

import jax
import jax.numpy as jnp
from jax import lax
from jax.experimental import pallas as pl
from jax.experimental.pallas import tpu as pltpu
from jax.sharding import PartitionSpec as P

MESH = pl.DeviceIdType.MESH
F32 = jnp.float32
BF16 = jnp.bfloat16
OB = 32
R = 8
SLABS = 4
GROUPS = 32
CHIPS = 16
ROWS = 128
LON = 1024
MEM = 8
MEMBERS = 256
TILE_ROWS = 4
ROW_BLOCKS = 8
TILE_BLOCKS = 32
ROW_OBS = ROW_BLOCKS * OB
TURN_ROWS = 16


def split(value):
    high = value.astype(BF16)
    low = (value - high.astype(F32)).astype(BF16)
    return high, low


def dot3(a_high, a_low, b_high, b_low):
    dot = functools.partial(jnp.dot, preferred_element_type=F32)
    return dot(a_high, b_high) + dot(a_high, b_low) + dot(a_low, b_high)


def dot_t(a, b):
    return lax.dot_general(a, b, (((1,), (1,)), ((), ())), preferred_element_type=F32)


def cycle_kernel(
    init_ref, sten_ref, inn_ref, prec_ref, cell_ref, band_ref, ret_ref,
    xbuf, xt, sten, coef, step_a, step_b, fsend, fields, anom_high, anom_low,
    pick, obs, obs_high, obs_low, wgt, wgt_high, wgt_low, inn, square, taper, upd,
    load_sem, halo_send, halo_recv, fwd_send, fwd_recv, own_sem, rim_send, rim_recv, ret_send, ret_recv,
):
    s = lax.axis_index("slab")
    g = lax.axis_index("member")
    chip = g // 2
    core = g % 2
    flat = s * GROUPS + g
    up = lax.rem(s + 1, SLABS)
    down = lax.rem(s + SLABS - 1, SLABS)
    nxt = lax.rem(flat + 1, SLABS * GROUPS)
    prv = lax.rem(flat + SLABS * GROUPS - 1, SLABS * GROUPS)
    nxt_id = (nxt // GROUPS, lax.rem(nxt, GROUPS))
    prv_id = (prv // GROUPS, lax.rem(prv, GROUPS))

    barrier = pltpu.get_barrier_semaphore()

    def greet(i, carry):
        peer = lax.rem(g + i, GROUPS)
        pl.semaphore_signal(barrier, inc=1, device_id=(s, peer), device_id_type=MESH)
        return carry

    for device in ((up, g), (down, g), nxt_id, prv_id):
        pl.semaphore_signal(barrier, inc=1, device_id=device, device_id_type=MESH)
    lax.fori_loop(1, GROUPS, greet, 0)

    load_x = pltpu.make_async_copy(init_ref, xbuf, load_sem.at[0])
    load_s = pltpu.make_async_copy(sten_ref, sten.at[:, pl.ds(8, ROWS), :], load_sem.at[1])
    load_i = pltpu.make_async_copy(inn_ref, inn, load_sem.at[2])
    load_x.start()
    load_s.start()
    load_i.start()

    load_x.wait()

    def turn(k, carry):
        start = pl.multiple_of(k * 8, 8)
        rows = xbuf[:, pl.ds(start, 8), :]
        xt[pl.ds(k * 8 + 4, 8)] = jnp.swapaxes(rows, 0, 1)
        return carry

    lax.fori_loop(0, CHIPS, turn, 0)

    def coefficients(start, live):
        rows = pl.ds(start, 8)
        k = sten[0, rows, :] * live
        u = sten[1, rows, :] * (0.5 * live)
        v = sten[2, rows, :] * (0.5 * live)
        coef[0, rows, :] = 1.0 - 4.0 * k
        coef[1, rows, :] = k - u
        coef[2, rows, :] = k + u
        coef[3, rows, :] = k - v
        coef[4, rows, :] = k + v

    load_s.wait()

    def own_coefficients(t, carry):
        coefficients(pl.multiple_of(t * 8 + 8, 8), 1.0)
        return carry

    lax.fori_loop(0, CHIPS, own_coefficients, 0)

    def remote(src, dst, send_sem, recv_sem, device):
        return pltpu.make_async_remote_copy(
            src_ref=src, dst_ref=dst, send_sem=send_sem, recv_sem=recv_sem,
            device_id=device, device_id_type=MESH,
        )

    halos = [
        remote(sten_ref.at[:, pl.ds(ROWS - 8, 8), :], sten.at[:, pl.ds(0, 8), :], halo_send.at[0], halo_recv.at[0], (up, g)),
        remote(sten_ref.at[:, pl.ds(0, 8), :], sten.at[:, pl.ds(ROWS + 8, 8), :], halo_send.at[1], halo_recv.at[1], (down, g)),
        remote(xt.at[pl.ds(ROWS, 4)], xt.at[pl.ds(0, 4)], halo_send.at[2], halo_recv.at[2], (up, g)),
        remote(xt.at[pl.ds(4, 4)], xt.at[pl.ds(ROWS + 4, 4)], halo_send.at[3], halo_recv.at[3], (down, g)),
    ]

    def target(i):
        return lax.rem(chip + (7 + 2 * core) * i, CHIPS)

    def advance(src, src_start, dst, dst_start, count, coef_base, coef_offset):
        for row in range(count):
            centre = src[src_start + row + 1]
            north = src[src_start + row + 2]
            south = src[src_start + row]
            east = pltpu.roll(centre, LON - 1, 1)
            west = pltpu.roll(centre, 1, 1)
            at = pl.ds(coef_base + coef_offset + row, 1)
            dst[dst_start + row] = (
                coef[0, at, :] * centre
                + coef[1, at, :] * east
                + coef[2, at, :] * west
                + coef[3, at, :] * north
                + coef[4, at, :] * south
            )

    def forecast(k):
        base = pl.multiple_of(k * 8, 8)
        advance(xt, k * 8, step_a, 0, 14, base, 5)
        advance(step_a, 0, step_b, 0, 12, base, 6)
        advance(step_b, 0, step_a, 0, 10, base, 7)
        advance(step_a, 0, fsend, k * 8, 8, base, 8)

    def send_rows(k, c, row, count, sem):
        remote(
            fsend.at[pl.ds(k * 8 + 4 * c + row, count)],
            fields.at[pl.ds(row, count), pl.ds(pl.multiple_of(g * MEM, MEM), MEM), :],
            fwd_send, sem, (s, 2 * k + c),
        ).start()

    def half(t):
        row = t * TILE_ROWS
        advance(xt, row, step_a, 0, 10, row, 5)
        advance(step_a, 0, step_b, 0, 8, row, 6)
        advance(step_b, 0, step_a, 0, 6, row, 7)
        advance(step_a, 0, fsend, row, 4, row, 8)

    def send_row(k, c, row):
        send_rows(k, c, row, 1, fwd_recv.at[{0: 0, 3: 0, 1: 1, 2: 2}[row]])

    def is_inner(k):
        return (k > 0) & (k < CHIPS - 1)

    def first_rows(i, carry):
        k = target(i)
        inner = is_inner(k)

        @pl.when(inner)
        def _():
            forecast(k)

        @pl.when(k == 0)
        def _():
            half(1)

        @pl.when(k == CHIPS - 1)
        def _():
            half(GROUPS - 2)

        @pl.when(i == 1)
        def _():
            pl.semaphore_wait(barrier, GROUPS - 1 + 4)
            for copy in halos:
                copy.start()

        @pl.when(inner)
        def _():
            for c in range(2):
                send_row(k, c, 0)
                send_row(k, c, 3)

        @pl.when(jnp.logical_not(inner))
        def _():
            for row in (0, 3, 1, 2):
                send_row(k, 1 - k // (CHIPS - 1), row)

        return carry

    lax.fori_loop(1, CHIPS, first_rows, 0)

    for copy in halos:
        copy.wait()
    coefficients(0, jnp.where(s == 0, 0.0, 1.0).astype(F32))
    coefficients(ROWS + 8, jnp.where(s == SLABS - 1, 0.0, 1.0).astype(F32))

    @pl.when(s == 0)
    def _():
        xt[pl.ds(0, 4)] = jnp.zeros((4, MEM, LON), F32)

    @pl.when(s == SLABS - 1)
    def _():
        xt[pl.ds(ROWS + 4, 4)] = jnp.zeros((4, MEM, LON), F32)

    half(0)
    half(GROUPS - 1)

    @pl.when(is_inner(chip))
    def _():
        forecast(chip)

    @pl.when(chip == 0)
    def _():
        half(1)

    @pl.when(chip == CHIPS - 1)
    def _():
        half(GROUPS - 2)

    for row in (0, 3):
        send_row(chip, 1 - core, row)
    own = pltpu.make_async_copy(
        fsend.at[pl.ds(g * 4, 4)], fields.at[:, pl.ds(pl.multiple_of(g * MEM, MEM), MEM), :], own_sem.at[0]
    )
    own.start()

    for row, border_rows in ((1, (0, 3)), (2, (1, 2))):
        def others(i, carry, row=row, border_rows=border_rows):
            k = target(i)

            @pl.when(is_inner(k))
            def _():
                for c in range(2):
                    send_row(k, c, row)

            @pl.when(jnp.logical_not(is_inner(k)))
            def _():
                for border_row in border_rows:
                    send_row(k, k // (CHIPS - 1), border_row)

            return carry

        lax.fori_loop(1, CHIPS, others, 0)
        send_row(chip, 1 - core, row)

    load_i.wait()
    scale = 1.0 / ((R + 1.0) * (MEMBERS - 1.0))
    for row in range(TILE_ROWS):
        cols = pl.ds(row * ROW_OBS, ROW_OBS)
        wgt[row + 1] = inn[:, cols] * (prec_ref[:, cols] * scale)

    def split_weights(slot):
        wgt_high[slot], wgt_low[slot] = split(wgt[slot])

    def split_observed(slot):
        obs_high[slot], obs_low[slot] = split(obs[slot])

    def send_rim(array, src, dst, n, device):
        def piece(p, carry):
            part = pl.ds(pl.multiple_of(p * OB, OB), OB)
            remote(array.at[src, part], array.at[dst, part], rim_send.at[n], rim_recv.at[n], device).start()
            return carry

        lax.fori_loop(0, ROW_OBS // OB, piece, 0)

    def rim_wait(array, sem):
        pltpu.make_async_copy(array.at[0], array.at[0], sem).wait()


    for row in range(TILE_ROWS):
        split_weights(row + 1)

    square[...] = jnp.zeros_like(square)
    square[pl.ds(0, TILE_BLOCKS), pl.ds(0, OB)] = cell_ref[...].astype(F32)
    cells = square[...].T
    lane = lax.broadcasted_iota(jnp.int32, (OB, 128), 1).astype(F32)
    for b in range(TILE_BLOCKS):
        pick[b] = jnp.where(lane == cells[:OB, b : b + 1], 1.0, 0.0).astype(BF16)

    block = lax.broadcasted_iota(jnp.int32, (128, TILE_BLOCKS), 1)
    slot_row = lax.broadcasted_iota(jnp.int32, (128, TILE_BLOCKS), 0)
    here = flat * TILE_BLOCKS + block
    row_start = flat * TILE_BLOCKS + jnp.bitwise_and(block, -8) - R
    total = jnp.zeros((128, TILE_BLOCKS), F32)
    for n in range(R + 1):
        chosen = band_ref[n : n + 1, :]
        height = (R + 1.0) - jnp.abs(chosen - here).astype(F32)
        total = total + jnp.where(slot_row == chosen - row_start, height, 0.0)
    square[:, pl.ds(0, TILE_BLOCKS)] = total
    taper[...] = square[...].T[:TILE_BLOCKS]

    own.wait()

    def prepare(row):
        def columns(c, carry):
            cols = pl.ds(pl.multiple_of(c * 256, 256), 256)
            field = fields[row, :, cols]
            mean = jnp.sum(field, axis=0, keepdims=True) * (1.0 / MEMBERS)
            high, low = split(field - mean)
            anom_high[row, :, cols] = high
            anom_low[row, :, cols] = low
            for b in range(2):
                pair = pl.ds(pl.multiple_of(c * 64 + b * OB, OB), OB)
                chosen = pick[row * ROW_BLOCKS + c * 2 + b]
                part = slice(b * 128, b * 128 + 128)
                obs[row + 1, pair, :] = dot_t(chosen, high[:, part]) + dot_t(chosen, low[:, part])
            return carry

        lax.fori_loop(0, 4, columns, 0)
        split_observed(row + 1)

    def arrived(row, count, sem):
        view = fields.at[pl.ds(row, count), pl.ds(0, MEMBERS - MEM), :]
        pltpu.make_async_copy(view, view, sem).wait()

    def analyse(row, parts=(0, 1, 2), begun=False):
        def columns(c, carry):
            cols = pl.ds(pl.multiple_of(c * 256, 256), 256)
            high = anom_high[row, :, cols]
            low = anom_low[row, :, cols]
            weights = [taper[pl.ds(row * ROW_BLOCKS + c * 2 + b, 1), :] for b in range(2)]
            total = (upd if begun else fields)[row, :, cols]
            for part in parts:
                slot = row + part
                cross = dot3(obs_high[slot], obs_low[slot], high, low)
                spread = jnp.concatenate(
                    [
                        jnp.concatenate(
                            [
                                jnp.broadcast_to(weights[b][:, part * 8 + j : part * 8 + j + 1], (OB, 128))
                                for b in range(2)
                            ],
                            axis=1,
                        )
                        for j in range(8)
                    ],
                    axis=0,
                )
                cross_high, cross_low = split(cross * spread)
                total = total + dot3(wgt_high[slot], wgt_low[slot], cross_high, cross_low)
            upd[row, :, cols] = total
            return carry

        lax.fori_loop(0, 4, columns, 0)

    def give_back(row):
        def one(k, c):
            d = 2 * k + c
            remote(
                upd.at[row, pl.ds(pl.multiple_of(d * MEM, MEM), MEM), :], ret_ref.at[TILE_ROWS * g + row],
                ret_send, ret_recv, (s, d),
            ).start()

        def others(i, carry):
            k = target(CHIPS - i)
            for c in range(2):
                one(k, c)
            return carry

        lax.fori_loop(1, CHIPS, others, 0)
        one(chip, 1 - core)

    arrived(0, 2, fwd_recv.at[0])

    def prepare_first(t, carry):
        @pl.when(t == 2)
        def _():
            arrived(1, 1, fwd_recv.at[1])

        prepare(jnp.where(t == 1, TILE_ROWS - 1, t // 2))
        return carry

    lax.fori_loop(0, 3, prepare_first, 0)
    analyse(1, (0, 1))

    arrived(2, 1, fwd_recv.at[2])
    for array, n in ((obs, 2), (wgt, 0)):
        send_rim(array, TILE_ROWS, 0, n, nxt_id)
        send_rim(array, 1, TILE_ROWS + 1, n + 1, prv_id)
    prepare(2)
    analyse(1, (2,), begun=True)
    give_back(1)

    def finish(t, carry):
        @pl.when(t == 1)
        def _():
            for n in range(2):
                rim_wait(wgt, rim_recv.at[n])
                rim_wait(obs, rim_recv.at[n + 2])
            for slot in (0, TILE_ROWS + 1):
                split_weights(slot)
                split_observed(slot)

        row = jnp.where(t == 0, 2, (t - 1) * (TILE_ROWS - 1))
        analyse(row)
        give_back(row)
        return carry

    lax.fori_loop(0, 3, finish, 0)

    keep = pltpu.make_async_copy(
        upd.at[:, pl.ds(pl.multiple_of(g * MEM, MEM), MEM), :], ret_ref.at[pl.ds(TILE_ROWS * g, TILE_ROWS)], own_sem.at[1]
    )
    keep.start()
    for n in range(4):
        rim_wait(wgt, rim_send.at[n])
    sent = fsend.at[pl.ds(0, ROWS - 4)]
    pltpu.make_async_copy(sent, sent, fwd_send).wait()
    keep.wait()
    back = ret_ref.at[pl.ds(0, ROWS - 4)]
    pltpu.make_async_copy(back, back, ret_send).wait()
    pltpu.make_async_copy(back, back, ret_recv).wait()


def turn_kernel(rows_ref, out_ref, rows, turned, load_sem, store_sem):
    def load(n):
        part = pl.ds(n * TURN_ROWS, TURN_ROWS)
        return pltpu.make_async_copy(rows_ref.at[part], rows.at[part], load_sem.at[n])

    def store(n):
        part = pl.ds(n * TURN_ROWS, TURN_ROWS)
        return pltpu.make_async_copy(turned.at[:, part, :], out_ref.at[:, part, :], store_sem.at[n])

    count = ROWS // TURN_ROWS
    for n in range(count):
        load(n).start()
    for n in range(count):
        load(n).wait()
        for start in range(n * TURN_ROWS, (n + 1) * TURN_ROWS, 8):
            turned[:, pl.ds(start, 8), :] = jnp.swapaxes(rows[pl.ds(start, 8)], 0, 1)
        store(n).start()
    for n in range(count):
        store(n).wait()


def shards(initial, stencil_numbers, innovations, obs_prec, obs_cell, band_idx):
    vmem = pl.BlockSpec(memory_space=pltpu.VMEM)
    hbm = pl.BlockSpec(memory_space=pl.ANY)
    dma = pltpu.SemaphoreType.DMA
    rows = pl.pallas_call(
        cycle_kernel,
        out_shape=jax.ShapeDtypeStruct((ROWS, MEM, LON), F32),
        in_specs=[hbm, hbm, hbm, vmem, vmem, vmem],
        out_specs=hbm,
        scratch_shapes=[
            pltpu.VMEM((MEM, ROWS, LON), F32),
            pltpu.VMEM((ROWS + 8, MEM, LON), F32),
            pltpu.VMEM((3, ROWS + 16, LON), F32),
            pltpu.VMEM((5, ROWS + 16, LON), F32),
            pltpu.VMEM((14, MEM, LON), F32),
            pltpu.VMEM((14, MEM, LON), F32),
            pltpu.VMEM((ROWS, MEM, LON), F32),
            pltpu.VMEM((TILE_ROWS, MEMBERS, LON), F32),
            pltpu.VMEM((TILE_ROWS, MEMBERS, LON), BF16),
            pltpu.VMEM((TILE_ROWS, MEMBERS, LON), BF16),
            pltpu.VMEM((TILE_BLOCKS, OB, 128), BF16),
            pltpu.VMEM((TILE_ROWS + 2, ROW_OBS, MEMBERS), F32),
            pltpu.VMEM((TILE_ROWS + 2, ROW_OBS, MEMBERS), BF16),
            pltpu.VMEM((TILE_ROWS + 2, ROW_OBS, MEMBERS), BF16),
            pltpu.VMEM((TILE_ROWS + 2, MEMBERS, ROW_OBS), F32),
            pltpu.VMEM((TILE_ROWS + 2, MEMBERS, ROW_OBS), BF16),
            pltpu.VMEM((TILE_ROWS + 2, MEMBERS, ROW_OBS), BF16),
            pltpu.VMEM((MEMBERS, TILE_ROWS * ROW_OBS), F32),
            pltpu.VMEM((128, 128), F32),
            pltpu.VMEM((TILE_BLOCKS, 128), F32),
            pltpu.VMEM((TILE_ROWS, MEMBERS, LON), F32),
            dma((3,)),
            dma((4,)),
            dma((4,)),
            dma(()),
            dma((3,)),
            dma((2,)),
            dma((4,)),
            dma((4,)),
            dma(()),
            dma(()),
        ],
        compiler_params=pltpu.CompilerParams(
            collective_id=0, has_side_effects=True, vmem_limit_bytes=60 * 2**20
        ),
        name="cycle",
    )(initial, stencil_numbers, innovations, obs_prec.reshape(1, -1), obs_cell, band_idx.T)
    return pl.pallas_call(
        turn_kernel,
        out_shape=jax.ShapeDtypeStruct((MEM, ROWS, LON), F32),
        in_specs=[hbm],
        out_specs=hbm,
        scratch_shapes=[
            pltpu.VMEM((ROWS, MEM, LON), F32),
            pltpu.VMEM((MEM, ROWS, LON), F32),
            dma((ROWS // TURN_ROWS,)),
            dma((ROWS // TURN_ROWS,)),
        ],
        compiler_params=pltpu.CompilerParams(vmem_limit_bytes=60 * 2**20),
        name="turn",
    )(rows)


def solution(mesh):
    in_specs = (
        P("member", "slab", None),
        P(None, "slab", None),
        P(None, ("slab", "member")),
        P(("slab", "member")),
        P(("slab", "member"), None),
        P(("slab", "member"), None),
    )
    out_specs = P("member", "slab", None)
    return jax.shard_map(shards, mesh=mesh, in_specs=in_specs, out_specs=out_specs, check_vma=False)
```

```python
import functools

import jax
import jax.numpy as jnp
from jax import lax
from jax.experimental import pallas as pl
from jax.experimental.pallas import tpu as pltpu
from jax.sharding import PartitionSpec as P

MESH = pl.DeviceIdType.MESH
F32 = jnp.float32
BF16 = jnp.bfloat16
OB = 32
R = 8
SLABS = 4
GROUPS = 32
CHIPS = 16
ROWS = 128
LON = 1024
MEM = 8
MEMBERS = 256
TILE_ROWS = 4
ROW_BLOCKS = 8
TILE_BLOCKS = 32
ROW_OBS = ROW_BLOCKS * OB
TURN_ROWS = 16


def split(value):
    high = value.astype(BF16)
    low = (value - high.astype(F32)).astype(BF16)
    return high, low


def dot3(a_high, a_low, b_high, b_low):
    dot = functools.partial(jnp.dot, preferred_element_type=F32)
    return dot(a_high, b_high) + dot(a_high, b_low) + dot(a_low, b_high)


def dot_t(a, b):
    return lax.dot_general(a, b, (((1,), (1,)), ((), ())), preferred_element_type=F32)


def cycle_kernel(
    init_ref, sten_ref, inn_ref, prec_ref, cell_ref, band_ref, ret_ref,
    xbuf, xt, sten, coef, step_a, step_b, fsend, fields, anom_high, anom_low,
    pick, obs, obs_high, obs_low, wgt, wgt_high, wgt_low, inn, square, taper, upd,
    load_sem, halo_send, halo_recv, fwd_send, fwd_recv, own_sem, rim_send, rim_recv, ret_send, ret_recv,
):
    s = lax.axis_index("slab")
    g = lax.axis_index("member")
    chip = g // 2
    core = g % 2
    flat = s * GROUPS + g
    up = lax.rem(s + 1, SLABS)
    down = lax.rem(s + SLABS - 1, SLABS)
    nxt = lax.rem(flat + 1, SLABS * GROUPS)
    prv = lax.rem(flat + SLABS * GROUPS - 1, SLABS * GROUPS)
    nxt_id = (nxt // GROUPS, lax.rem(nxt, GROUPS))
    prv_id = (prv // GROUPS, lax.rem(prv, GROUPS))

    barrier = pltpu.get_barrier_semaphore()

    def greet(i, carry):
        peer = lax.rem(g + i, GROUPS)
        pl.semaphore_signal(barrier, inc=1, device_id=(s, peer), device_id_type=MESH)
        return carry

    for device in ((up, g), (down, g), nxt_id, prv_id):
        pl.semaphore_signal(barrier, inc=1, device_id=device, device_id_type=MESH)
    lax.fori_loop(1, GROUPS, greet, 0)

    load_x = pltpu.make_async_copy(init_ref, xbuf, load_sem.at[0])
    load_s = pltpu.make_async_copy(sten_ref, sten.at[:, pl.ds(8, ROWS), :], load_sem.at[1])
    load_i = pltpu.make_async_copy(inn_ref, inn, load_sem.at[2])
    load_x.start()
    load_s.start()
    load_i.start()

    load_x.wait()

    def turn(k, carry):
        start = pl.multiple_of(k * 8, 8)
        rows = xbuf[:, pl.ds(start, 8), :]
        xt[pl.ds(k * 8 + 4, 8)] = jnp.swapaxes(rows, 0, 1)
        return carry

    lax.fori_loop(0, CHIPS, turn, 0)

    def coefficients(start, live):
        rows = pl.ds(start, 8)
        k = sten[0, rows, :] * live
        u = sten[1, rows, :] * (0.5 * live)
        v = sten[2, rows, :] * (0.5 * live)
        coef[0, rows, :] = 1.0 - 4.0 * k
        coef[1, rows, :] = k - u
        coef[2, rows, :] = k + u
        coef[3, rows, :] = k - v
        coef[4, rows, :] = k + v

    load_s.wait()

    def own_coefficients(t, carry):
        coefficients(pl.multiple_of(t * 8 + 8, 8), 1.0)
        return carry

    lax.fori_loop(0, CHIPS, own_coefficients, 0)

    def remote(src, dst, send_sem, recv_sem, device):
        return pltpu.make_async_remote_copy(
            src_ref=src, dst_ref=dst, send_sem=send_sem, recv_sem=recv_sem,
            device_id=device, device_id_type=MESH,
        )

    halos = [
        remote(sten_ref.at[:, pl.ds(ROWS - 8, 8), :], sten.at[:, pl.ds(0, 8), :], halo_send.at[0], halo_recv.at[0], (up, g)),
        remote(sten_ref.at[:, pl.ds(0, 8), :], sten.at[:, pl.ds(ROWS + 8, 8), :], halo_send.at[1], halo_recv.at[1], (down, g)),
        remote(xt.at[pl.ds(ROWS, 4)], xt.at[pl.ds(0, 4)], halo_send.at[2], halo_recv.at[2], (up, g)),
        remote(xt.at[pl.ds(4, 4)], xt.at[pl.ds(ROWS + 4, 4)], halo_send.at[3], halo_recv.at[3], (down, g)),
    ]

    def target(i):
        return lax.rem(chip + (7 + 2 * core) * i, CHIPS)

    def advance(src, src_start, dst, dst_start, count, coef_base, coef_offset):
        for row in range(count):
            centre = src[src_start + row + 1]
            north = src[src_start + row + 2]
            south = src[src_start + row]
            east = pltpu.roll(centre, LON - 1, 1)
            west = pltpu.roll(centre, 1, 1)
            at = pl.ds(coef_base + coef_offset + row, 1)
            dst[dst_start + row] = (
                coef[0, at, :] * centre
                + coef[1, at, :] * east
                + coef[2, at, :] * west
                + coef[3, at, :] * north
                + coef[4, at, :] * south
            )

    def forecast(k):
        base = pl.multiple_of(k * 8, 8)
        advance(xt, k * 8, step_a, 0, 14, base, 5)
        advance(step_a, 0, step_b, 0, 12, base, 6)
        advance(step_b, 0, step_a, 0, 10, base, 7)
        advance(step_a, 0, fsend, k * 8, 8, base, 8)

    def send_rows(k, c, row, count, sem):
        remote(
            fsend.at[pl.ds(k * 8 + 4 * c + row, count)],
            fields.at[pl.ds(row, count), pl.ds(pl.multiple_of(g * MEM, MEM), MEM), :],
            fwd_send, sem, (s, 2 * k + c),
        ).start()

    def half(t):
        row = t * TILE_ROWS
        advance(xt, row, step_a, 0, 10, row, 5)
        advance(step_a, 0, step_b, 0, 8, row, 6)
        advance(step_b, 0, step_a, 0, 6, row, 7)
        advance(step_a, 0, fsend, row, 4, row, 8)

    def send_row(k, c, row):
        send_rows(k, c, row, 1, fwd_recv.at[{0: 0, 3: 0, 1: 1, 2: 2}[row]])

    def is_inner(k):
        return (k > 0) & (k < CHIPS - 1)

    def first_rows(i, carry):
        k = target(i)
        inner = is_inner(k)

        @pl.when(inner)
        def _():
            forecast(k)

        @pl.when(k == 0)
        def _():
            half(1)

        @pl.when(k == CHIPS - 1)
        def _():
            half(GROUPS - 2)

        @pl.when(i == 1)
        def _():
            pl.semaphore_wait(barrier, GROUPS - 1 + 4)
            for copy in halos:
                copy.start()

        @pl.when(inner)
        def _():
            for c in range(2):
                send_row(k, c, 0)
                send_row(k, c, 3)

        @pl.when(jnp.logical_not(inner))
        def _():
            for row in (0, 3, 1, 2):
                send_row(k, 1 - k // (CHIPS - 1), row)

        return carry

    lax.fori_loop(1, CHIPS, first_rows, 0)

    for copy in halos:
        copy.wait()
    coefficients(0, jnp.where(s == 0, 0.0, 1.0).astype(F32))
    coefficients(ROWS + 8, jnp.where(s == SLABS - 1, 0.0, 1.0).astype(F32))

    @pl.when(s == 0)
    def _():
        xt[pl.ds(0, 4)] = jnp.zeros((4, MEM, LON), F32)

    @pl.when(s == SLABS - 1)
    def _():
        xt[pl.ds(ROWS + 4, 4)] = jnp.zeros((4, MEM, LON), F32)

    half(0)
    half(GROUPS - 1)

    @pl.when(is_inner(chip))
    def _():
        forecast(chip)

    @pl.when(chip == 0)
    def _():
        half(1)

    @pl.when(chip == CHIPS - 1)
    def _():
        half(GROUPS - 2)

    for row in (0, 3):
        send_row(chip, 1 - core, row)
    own = pltpu.make_async_copy(
        fsend.at[pl.ds(g * 4, 4)], fields.at[:, pl.ds(pl.multiple_of(g * MEM, MEM), MEM), :], own_sem.at[0]
    )
    own.start()

    for row, border_rows in ((1, (0, 3)), (2, (1, 2))):
        def others(i, carry, row=row, border_rows=border_rows):
            k = target(i)

            @pl.when(is_inner(k))
            def _():
                for c in range(2):
                    send_row(k, c, row)

            @pl.when(jnp.logical_not(is_inner(k)))
            def _():
                for border_row in border_rows:
                    send_row(k, k // (CHIPS - 1), border_row)

            return carry

        lax.fori_loop(1, CHIPS, others, 0)
        send_row(chip, 1 - core, row)

    load_i.wait()
    scale = 1.0 / ((R + 1.0) * (MEMBERS - 1.0))
    for row in range(TILE_ROWS):
        cols = pl.ds(row * ROW_OBS, ROW_OBS)
        wgt[row + 1] = inn[:, cols] * (prec_ref[:, cols] * scale)

    def split_weights(slot):
        wgt_high[slot], wgt_low[slot] = split(wgt[slot])

    def split_observed(slot):
        obs_high[slot], obs_low[slot] = split(obs[slot])

    def send_rim(array, src, dst, n, device):
        def piece(p, carry):
            part = pl.ds(pl.multiple_of(p * OB, OB), OB)
            remote(array.at[src, part], array.at[dst, part], rim_send.at[n], rim_recv.at[n], device).start()
            return carry

        lax.fori_loop(0, ROW_OBS // OB, piece, 0)

    def rim_wait(array, sem):
        pltpu.make_async_copy(array.at[0], array.at[0], sem).wait()


    for row in range(TILE_ROWS):
        split_weights(row + 1)

    square[...] = jnp.zeros_like(square)
    square[pl.ds(0, TILE_BLOCKS), pl.ds(0, OB)] = cell_ref[...].astype(F32)
    cells = square[...].T
    lane = lax.broadcasted_iota(jnp.int32, (OB, 128), 1).astype(F32)
    for b in range(TILE_BLOCKS):
        pick[b] = jnp.where(lane == cells[:OB, b : b + 1], 1.0, 0.0).astype(BF16)

    block = lax.broadcasted_iota(jnp.int32, (128, TILE_BLOCKS), 1)
    slot_row = lax.broadcasted_iota(jnp.int32, (128, TILE_BLOCKS), 0)
    here = flat * TILE_BLOCKS + block
    row_start = flat * TILE_BLOCKS + jnp.bitwise_and(block, -8) - R
    total = jnp.zeros((128, TILE_BLOCKS), F32)
    for n in range(R + 1):
        chosen = band_ref[n : n + 1, :]
        height = (R + 1.0) - jnp.abs(chosen - here).astype(F32)
        total = total + jnp.where(slot_row == chosen - row_start, height, 0.0)
    square[:, pl.ds(0, TILE_BLOCKS)] = total
    taper[...] = square[...].T[:TILE_BLOCKS]

    own.wait()

    def prepare(row):
        def columns(c, carry):
            cols = pl.ds(pl.multiple_of(c * 256, 256), 256)
            field = fields[row, :, cols]
            mean = jnp.sum(field, axis=0, keepdims=True) * (1.0 / MEMBERS)
            high, low = split(field - mean)
            anom_high[row, :, cols] = high
            anom_low[row, :, cols] = low
            for b in range(2):
                pair = pl.ds(pl.multiple_of(c * 64 + b * OB, OB), OB)
                chosen = pick[row * ROW_BLOCKS + c * 2 + b]
                part = slice(b * 128, b * 128 + 128)
                obs[row + 1, pair, :] = dot_t(chosen, high[:, part]) + dot_t(chosen, low[:, part])
            return carry

        lax.fori_loop(0, 4, columns, 0)
        split_observed(row + 1)

    def arrived(row, count, sem):
        view = fields.at[pl.ds(row, count), pl.ds(0, MEMBERS - MEM), :]
        pltpu.make_async_copy(view, view, sem).wait()

    def analyse(row, parts=(0, 1, 2), begun=False):
        def columns(c, carry):
            cols = pl.ds(pl.multiple_of(c * 256, 256), 256)
            high = anom_high[row, :, cols]
            low = anom_low[row, :, cols]
            weights = [taper[pl.ds(row * ROW_BLOCKS + c * 2 + b, 1), :] for b in range(2)]
            total = (upd if begun else fields)[row, :, cols]
            for part in parts:
                slot = row + part
                cross = dot3(obs_high[slot], obs_low[slot], high, low)
                spread = jnp.concatenate(
                    [
                        jnp.concatenate(
                            [
                                jnp.broadcast_to(weights[b][:, part * 8 + j : part * 8 + j + 1], (OB, 128))
                                for b in range(2)
                            ],
                            axis=1,
                        )
                        for j in range(8)
                    ],
                    axis=0,
                )
                cross_high, cross_low = split(cross * spread)
                total = total + dot3(wgt_high[slot], wgt_low[slot], cross_high, cross_low)
            upd[row, :, cols] = total
            return carry

        lax.fori_loop(0, 4, columns, 0)

    def give_back(row):
        def one(k, c):
            d = 2 * k + c
            remote(
                upd.at[row, pl.ds(pl.multiple_of(d * MEM, MEM), MEM), :], ret_ref.at[TILE_ROWS * g + row],
                ret_send, ret_recv, (s, d),
            ).start()

        def others(i, carry):
            k = target(CHIPS - i)
            for c in range(2):
                one(k, c)
            return carry

        lax.fori_loop(1, CHIPS, others, 0)
        one(chip, 1 - core)

    arrived(0, 2, fwd_recv.at[0])

    def prepare_first(t, carry):
        @pl.when(t == 2)
        def _():
            arrived(1, 1, fwd_recv.at[1])

        prepare(jnp.where(t == 1, TILE_ROWS - 1, t // 2))
        return carry

    lax.fori_loop(0, 3, prepare_first, 0)
    for array, n in ((wgt, 0),):
        send_rim(array, TILE_ROWS, 0, n, nxt_id)
        send_rim(array, 1, TILE_ROWS + 1, n + 1, prv_id)
    analyse(1, (0, 1))

    arrived(2, 1, fwd_recv.at[2])
    for array, n in ((obs, 2),):
        send_rim(array, TILE_ROWS, 0, n, nxt_id)
        send_rim(array, 1, TILE_ROWS + 1, n + 1, prv_id)
    prepare(2)
    analyse(1, (2,), begun=True)
    give_back(1)

    def finish(t, carry):
        @pl.when(t == 1)
        def _():
            for n in range(2):
                rim_wait(wgt, rim_recv.at[n])
                rim_wait(obs, rim_recv.at[n + 2])
            for slot in (0, TILE_ROWS + 1):
                split_weights(slot)
                split_observed(slot)

        row = jnp.where(t == 0, 2, (t - 1) * (TILE_ROWS - 1))
        analyse(row)
        give_back(row)
        return carry

    lax.fori_loop(0, 3, finish, 0)

    keep = pltpu.make_async_copy(
        upd.at[:, pl.ds(pl.multiple_of(g * MEM, MEM), MEM), :], ret_ref.at[pl.ds(TILE_ROWS * g, TILE_ROWS)], own_sem.at[1]
    )
    keep.start()
    for n in range(4):
        rim_wait(wgt, rim_send.at[n])
    sent = fsend.at[pl.ds(0, ROWS - 4)]
    pltpu.make_async_copy(sent, sent, fwd_send).wait()
    keep.wait()
    back = ret_ref.at[pl.ds(0, ROWS - 4)]
    pltpu.make_async_copy(back, back, ret_send).wait()
    pltpu.make_async_copy(back, back, ret_recv).wait()


def turn_kernel(rows_ref, out_ref, rows, turned, load_sem, store_sem):
    def load(n):
        part = pl.ds(n * TURN_ROWS, TURN_ROWS)
        return pltpu.make_async_copy(rows_ref.at[part], rows.at[part], load_sem.at[n])

    def store(n):
        part = pl.ds(n * TURN_ROWS, TURN_ROWS)
        return pltpu.make_async_copy(turned.at[:, part, :], out_ref.at[:, part, :], store_sem.at[n])

    count = ROWS // TURN_ROWS
    for n in range(count):
        load(n).start()
    for n in range(count):
        load(n).wait()
        for start in range(n * TURN_ROWS, (n + 1) * TURN_ROWS, 8):
            turned[:, pl.ds(start, 8), :] = jnp.swapaxes(rows[pl.ds(start, 8)], 0, 1)
        store(n).start()
    for n in range(count):
        store(n).wait()


def shards(initial, stencil_numbers, innovations, obs_prec, obs_cell, band_idx):
    vmem = pl.BlockSpec(memory_space=pltpu.VMEM)
    hbm = pl.BlockSpec(memory_space=pl.ANY)
    dma = pltpu.SemaphoreType.DMA
    rows = pl.pallas_call(
        cycle_kernel,
        out_shape=jax.ShapeDtypeStruct((ROWS, MEM, LON), F32),
        in_specs=[hbm, hbm, hbm, vmem, vmem, vmem],
        out_specs=hbm,
        scratch_shapes=[
            pltpu.VMEM((MEM, ROWS, LON), F32),
            pltpu.VMEM((ROWS + 8, MEM, LON), F32),
            pltpu.VMEM((3, ROWS + 16, LON), F32),
            pltpu.VMEM((5, ROWS + 16, LON), F32),
            pltpu.VMEM((14, MEM, LON), F32),
            pltpu.VMEM((14, MEM, LON), F32),
            pltpu.VMEM((ROWS, MEM, LON), F32),
            pltpu.VMEM((TILE_ROWS, MEMBERS, LON), F32),
            pltpu.VMEM((TILE_ROWS, MEMBERS, LON), BF16),
            pltpu.VMEM((TILE_ROWS, MEMBERS, LON), BF16),
            pltpu.VMEM((TILE_BLOCKS, OB, 128), BF16),
            pltpu.VMEM((TILE_ROWS + 2, ROW_OBS, MEMBERS), F32),
            pltpu.VMEM((TILE_ROWS + 2, ROW_OBS, MEMBERS), BF16),
            pltpu.VMEM((TILE_ROWS + 2, ROW_OBS, MEMBERS), BF16),
            pltpu.VMEM((TILE_ROWS + 2, MEMBERS, ROW_OBS), F32),
            pltpu.VMEM((TILE_ROWS + 2, MEMBERS, ROW_OBS), BF16),
            pltpu.VMEM((TILE_ROWS + 2, MEMBERS, ROW_OBS), BF16),
            pltpu.VMEM((MEMBERS, TILE_ROWS * ROW_OBS), F32),
            pltpu.VMEM((128, 128), F32),
            pltpu.VMEM((TILE_BLOCKS, 128), F32),
            pltpu.VMEM((TILE_ROWS, MEMBERS, LON), F32),
            dma((3,)),
            dma((4,)),
            dma((4,)),
            dma(()),
            dma((3,)),
            dma((2,)),
            dma((4,)),
            dma((4,)),
            dma(()),
            dma(()),
        ],
        compiler_params=pltpu.CompilerParams(
            collective_id=0, has_side_effects=True, vmem_limit_bytes=60 * 2**20
        ),
        name="cycle",
    )(initial, stencil_numbers, innovations, obs_prec.reshape(1, -1), obs_cell, band_idx.T)
    return pl.pallas_call(
        turn_kernel,
        out_shape=jax.ShapeDtypeStruct((MEM, ROWS, LON), F32),
        in_specs=[hbm],
        out_specs=hbm,
        scratch_shapes=[
            pltpu.VMEM((ROWS, MEM, LON), F32),
            pltpu.VMEM((MEM, ROWS, LON), F32),
            dma((ROWS // TURN_ROWS,)),
            dma((ROWS // TURN_ROWS,)),
        ],
        compiler_params=pltpu.CompilerParams(vmem_limit_bytes=60 * 2**20),
        name="turn",
    )(rows)


def solution(mesh):
    in_specs = (
        P("member", "slab", None),
        P(None, "slab", None),
        P(None, ("slab", "member")),
        P(("slab", "member")),
        P(("slab", "member"), None),
        P(("slab", "member"), None),
    )
    out_specs = P("member", "slab", None)
    return jax.shard_map(shards, mesh=mesh, in_specs=in_specs, out_specs=out_specs, check_vma=False)
```
